32 devices in a mesh: prow: 2 (over core), pcol: 16 (over z, y, x).
Axes of the slice: x: 2, y: 2, z: 4, core: 2. Of those that a mesh axis runs over, the one named last changes fastest.
Arguments:
- factor_rows: float32 [8, 256, 24, 2048], P(None, 'prow', None, 'pcol'), as said below
- sensitivity: float32 [1024, 24, 2048], P('prow', None, 'pcol'), may hold values from -6 to 6
- pivots: int32 [2048], replicated, may hold values from 0 to 2047, as said below
Outputs:
- adjoint: float32 [1024, 8, 256], P(None, None, 'prow')
- updated: float32 [1024, 24, 2048], P('prow', None, 'pcol')
The draws below stay inside these ranges and needn't reach their ends.
Inputs may be any that keep to these rules, and one draw needn't show every extreme that they name: pivots is a permutation of the first 2048 columns. `factor_rows`: in M, the entries left of each block row's diagonal block are zero and each diagonal block is lower triangular.
All inputs are finite; a program needn't handle non-finite values.
Results may differ from the reference program's by a relative error of at most 0.0001.
Values sent between devices are 32-bit elements; how exact they have to be, the bound alone decides.
No kernel may reach another device: no remote copies, remote signals or barrier semaphores. Data moves between devices by JAX's collectives and lax.ppermute only.
A program may use at most 192 MiB of HBM per device.

```python
import math
import jax
import jax.numpy as jnp
from jax import lax

NB = 1024
TILE = 128
NRHS = 1024
CT_DEV = 24
SLAB = 256
STRIPE = 2048
RSW = 8
COLS = 49152


def draw_factor_rows(key, part):
    key_base, key_diag = jax.random.split(jax.random.fold_in(key, 11))
    total_rows = 2 * NB
    base_draw = jax.random.normal(key_base, (total_rows, COLS), jnp.float32)
    diag_vals = jax.random.uniform(key_diag, (total_rows, 1), jnp.float32, 1.0, 2.0)
    row_ids = jnp.arange(total_rows)[:, None]
    col_ids = jnp.arange(COLS)[None, :]
    row_block = row_ids // NB
    inner_row = row_ids % NB
    inner_col = col_ids % NB
    in_diag = col_ids // NB == row_block
    beyond = col_ids >= (row_block + 1) * NB
    lower_part = jnp.where(inner_col < inner_row, base_draw * (0.6 / math.sqrt(NB)), jnp.where(inner_col == inner_row, diag_vals, 0.0))
    values = jnp.where(in_diag, lower_part, jnp.where(beyond, base_draw / math.sqrt(2 * NB), 0.0))
    return values.reshape(RSW, SLAB, CT_DEV, STRIPE)


def shuffle_tile(tile_key):
    return jax.random.permutation(tile_key, TILE)


def draw_pivots(key, part):
    key_local, key_tiles, key_rank, key_count, key_mix = jax.random.split(jax.random.fold_in(key, 23), 5)
    tile_count = STRIPE // TILE
    local_order = jax.vmap(shuffle_tile)(jax.random.split(key_local, tile_count)).astype(jnp.int32)
    tile_order = jax.random.permutation(key_tiles, tile_count).astype(jnp.int32)
    base_cols = (tile_order[:, None] * TILE + local_order).reshape(STRIPE)
    mixed_count = jax.random.randint(key_count, (), 2, tile_count)
    tile_rank = jax.random.permutation(key_rank, tile_count)
    mixed_tile = tile_rank < mixed_count
    mixed_slot = jnp.repeat(mixed_tile, TILE, total_repeat_length=STRIPE)
    slot_ids = jnp.arange(STRIPE, dtype=jnp.int32)
    scramble = jax.random.permutation(key_mix, STRIPE).astype(jnp.int32)
    order_drawn = jnp.argsort(jnp.where(mixed_slot, slot_ids, STRIPE + slot_ids), stable=True)
    order_mixed = jnp.argsort(jnp.where(mixed_slot, scramble, STRIPE + slot_ids), stable=True)
    result = jnp.zeros((STRIPE,), jnp.int32).at[order_drawn].set(base_cols[order_mixed])
    return result


def block_levels(stream_key, extent, shards, low, largest):
    def one(dim, blocks):
        draws = jax.random.uniform(jax.random.fold_in(jax.random.fold_in(stream_key, 6), dim), (blocks,), jnp.float32, low / len(shards), largest / len(shards))
        return jnp.repeat(jnp.exp(draws), extent[dim] // blocks).reshape((-1,) + (1,) * (len(extent) - dim - 1))

    loudness = one(*shards[0])
    for cut in shards[1:]:
        loudness = loudness * one(*cut)
    return loudness


def normal_values(own_key, shape, deviation, most, cuts=(), kind=jnp.bfloat16):
    entries = jax.random.normal(own_key, shape, jnp.float32) * deviation
    if len(cuts) > 0:
        entries = block_levels(own_key, shape, cuts, -0.22, 0.18) * entries
    return jnp.clip(entries, min=-most, max=most).astype(kind)


def setup_inputs(seed: int = 0) -> dict:
    key_list = jax.random.split(jax.random.key(seed), 4)
    return {
        "factor_rows": draw_factor_rows(jax.random.fold_in(key_list[3], 71), 0),
        "sensitivity": normal_values(key_list[1], (NRHS, CT_DEV, STRIPE), 1.0, 6.0, ((0, 2), (2, 16)), jnp.float32),
        "pivots": draw_pivots(jax.random.fold_in(key_list[3], 71), 0),
    }


def reference(factor_rows, sensitivity, pivots):
    matrix = factor_rows.reshape(2 * NB, COLS)
    current = sensitivity.reshape(NRHS, COLS)
    swapped = jnp.take(current, pivots, axis=1)
    current = jnp.concatenate([swapped, current[:, STRIPE:]], axis=1)
    columns = jnp.arange(COLS)
    solved_list = []
    for section in range(2):
        block_rhs = current[:, section * NB:(section + 1) * NB]
        inverse_t = matrix[section * NB:(section + 1) * NB, section * NB:(section + 1) * NB]
        solved = jnp.dot(block_rhs, inverse_t.T, precision=lax.Precision.HIGHEST, preferred_element_type=jnp.float32)
        change = jnp.dot(solved, matrix[section * NB:(section + 1) * NB], precision=lax.Precision.HIGHEST, preferred_element_type=jnp.float32)
        current = current - jnp.where((columns >= (section + 1) * NB)[None, :], change, jnp.float32(0.0))
        solved_list.append(solved)
    adjoint = jnp.concatenate(solved_list, axis=1).reshape(NRHS, RSW, SLAB)
    return adjoint, current.reshape(NRHS, CT_DEV, STRIPE)
```

```python
import functools

import jax
import jax.numpy as jnp
from jax import lax
from jax.experimental import pallas as pl
from jax.experimental.pallas import tpu as pltpu
from jax.sharding import PartitionSpec as P

NB = 1024
F32 = jnp.float32
BF16 = jnp.bfloat16
VMEM_BYTES = 60 * 1024 * 1024


def grid_of(count):
    z_size = 4
    side = 1
    while side * side * z_size < count:
        side += 1
    return z_size, side, side


def split(value):
    high = value.astype(BF16)
    return high, (value - high.astype(F32)).astype(BF16)


def mul3(left, right, dims):
    dot = functools.partial(lax.dot_general, dimension_numbers=(dims, ((), ())), preferred_element_type=F32)
    return dot(left[0], right[0]) + (dot(left[0], right[1]) + dot(left[1], right[0]))


NN = ((1,), (0,))
NT = ((1,), (1,))


def shift(value, sizes, axis, step):
    z_size, y_size, x_size = sizes
    pairs = []
    for z in range(z_size):
        for y in range(y_size):
            for x in range(x_size):
                at = [z, y, x]
                to = list(at)
                to[axis] = (at[axis] + step) % sizes[axis]
                pairs.append(tuple((c[0] * y_size + c[1]) * x_size + c[2] for c in (at, to)))
    return lax.ppermute(value, "pcol", pairs)


def ring(value, sizes, axis):
    held = [value]
    for _ in range(sizes[axis] - 1):
        held.append(shift(held[-1], sizes, axis, 1))
    return held


def gather_pieces(block, sizes):
    half = block.shape[0] // 2
    pieces = []
    for dz, held in enumerate(ring(block, sizes, 0)):
        for dx, first in enumerate(ring(held[:half], sizes, 2)):
            for dy, second in enumerate(ring(first, sizes, 1)):
                pieces.append((0, (dz, dy, dx), second))
        for dy, first in enumerate(ring(held[half:], sizes, 1)):
            for dx, second in enumerate(ring(first, sizes, 2)):
                pieces.append((half, (dz, dy, dx), second))
    return pieces


def source_tiles(sizes, index):
    z_size, y_size, x_size = sizes
    z, y, x = index // (y_size * x_size), index // x_size % y_size, index % x_size
    places = jnp.arange(z_size * y_size * x_size)
    dz, dy, dx = places // (y_size * x_size), places // x_size % y_size, places % x_size
    return ((z - dz) % z_size * y_size + (y - dy) % y_size) * x_size + (x - dx) % x_size


def slot_of(place, sizes):
    return (place[0] * sizes[1] + place[1]) * sizes[2] + place[2]


def permute_columns(pieces, sizes, tiles, wanted, rows):
    count = sizes[0] * sizes[1] * sizes[2]
    width = wanted.shape[0]
    step = 256
    where = [(first, slot_of(place, sizes)) for first, place, _ in pieces]

    def kernel(tiles_ref, wanted_ref, *refs):
        parts, out_ref, high_ref, low_ref, hot_ref = refs[:-4], refs[-4], refs[-3], refs[-2], refs[-1]
        for (first, slot), part in zip(where, parts, strict=True):
            high, low = split(part[...])
            to = (pl.ds(first, part.shape[0]), pl.ds(slot * 128, 128))
            high_ref[to] = high
            low_ref[to] = low
        for start in range(0, width, step):
            size = min(step, width - start)
            columns = wanted_ref[:, pl.ds(start, size)]
            lane = lax.broadcasted_iota(jnp.int32, (128, size), 0)
            for slot in range(count):
                hot = (columns - tiles_ref[slot] * 128) == lane
                hot_ref[pl.ds(slot * 128, 128), pl.ds(0, size)] = hot.astype(F32).astype(BF16)
            hot = hot_ref[:, pl.ds(0, size)]
            dot = functools.partial(jnp.dot, preferred_element_type=F32)
            out_ref[:, pl.ds(start, size)] = dot(high_ref[...], hot) + dot(low_ref[...], hot)

    vmem = pl.BlockSpec(memory_space=pltpu.VMEM)
    return pl.pallas_call(
        kernel,
        out_shape=jax.ShapeDtypeStruct((rows, width), F32),
        in_specs=[pl.BlockSpec(memory_space=pltpu.SMEM), vmem] + [vmem] * len(pieces),
        out_specs=vmem,
        scratch_shapes=[
            pltpu.VMEM((rows, count * 128), BF16),
            pltpu.VMEM((rows, count * 128), BF16),
            pltpu.VMEM((count * 128, step), BF16),
        ],
        compiler_params=pltpu.CompilerParams(vmem_limit_bytes=VMEM_BYTES),
        name="permute_columns",
    )(tiles, wanted.reshape(1, width), *[p[2] for p in pieces])


def prepare(block, keep, name):
    cycles, depth, tiles, width = block.shape

    def kernel(keep_ref, in_ref, high_ref, low_ref):
        own = keep_ref[pl.program_id(0) // (cycles // 2)]
        for b in range(tiles):
            value = in_ref[0, pl.ds(b, depth, stride=tiles), :]
            if b == 0:
                value = jnp.where(own > 0, value, jnp.zeros_like(value))
            high, low = split(value)
            high_ref[:, pl.ds(b * width, width)] = high
            low_ref[:, pl.ds(b * width, width)] = low

    out = jax.ShapeDtypeStruct((cycles * depth, tiles * width), BF16)
    spec = pl.BlockSpec((depth, tiles * width), lambda a: (a, 0))
    return pl.pallas_call(
        kernel,
        grid=(cycles,),
        out_shape=(out, out),
        in_specs=[
            pl.BlockSpec(memory_space=pltpu.SMEM),
            pl.BlockSpec((1, depth * tiles, width), lambda a: (a, 0, 0)),
        ],
        out_specs=(spec, spec),
        compiler_params=pltpu.CompilerParams(vmem_limit_bytes=VMEM_BYTES),
        name=name,
    )(keep, block.reshape(cycles, depth * tiles, width))


def solve(rhs_offset, known, previous, stripe, coupling, diagonal):
    rows = stripe.shape[0]
    n_coupling = len(coupling)
    places = [(first, tile) for _, first, tile in coupling + diagonal]

    def kernel(*refs):
        refs = list(refs)
        stripe_ref = refs.pop(0)
        prev = (refs.pop(0), refs.pop(0)) if known else None
        parts = refs[: len(places)]
        out_ref, out_high, out_low, high_ref, low_ref, rhs_high, rhs_low = refs[len(places) :]

        def load(chosen):
            for (first, tile), part in chosen:
                high, low = split(part[...])
                to = (pl.ds(first, part.shape[0]), pl.ds(tile * 128, 128))
                high_ref[to] = high
                low_ref[to] = low

        pairs = list(zip(places, parts, strict=True))
        step = 256
        if known:
            load(pairs[:n_coupling])
            left = (prev[0][...], prev[1][...])
            for start in range(0, NB, step):
                to = (slice(None), pl.ds(start, step))
                value = stripe_ref[:, pl.ds(rhs_offset + start, step)] - mul3(left, (high_ref[to], low_ref[to]), NN)
                rhs_high[to], rhs_low[to] = split(value)
        else:
            for start in range(0, NB, step):
                to = (slice(None), pl.ds(start, step))
                rhs_high[to], rhs_low[to] = split(stripe_ref[:, pl.ds(rhs_offset + start, step)])
        load(pairs[n_coupling:])
        left = (rhs_high[...], rhs_low[...])
        for start in range(0, NB, step):
            to = (pl.ds(start, step), slice(None))
            value = mul3(left, (high_ref[to], low_ref[to]), NT)
            to = (slice(None), pl.ds(start, step))
            out_ref[to] = value
            out_high[to], out_low[to] = split(value)

    vmem = pl.BlockSpec(memory_space=pltpu.VMEM)
    operands = [stripe, *previous, *[c[0] for c in coupling + diagonal]]
    return pl.pallas_call(
        kernel,
        out_shape=(
            jax.ShapeDtypeStruct((rows, NB), F32),
            jax.ShapeDtypeStruct((rows, NB), BF16),
            jax.ShapeDtypeStruct((rows, NB), BF16),
        ),
        in_specs=[vmem] * len(operands),
        out_specs=(vmem, vmem, vmem),
        scratch_shapes=[pltpu.VMEM((NB, NB), BF16)] * 2 + [pltpu.VMEM((rows, NB), BF16)] * 2,
        compiler_params=pltpu.CompilerParams(vmem_limit_bytes=VMEM_BYTES),
        name="solve_second" if known else "solve_first",
    )(*operands)


def trail_first(sensitivity, own_tile, solved, halves):
    rows, tiles, width = sensitivity.shape
    group = 8

    def kernel(sens_ref, own_ref, yh_ref, yl_ref, ah_ref, al_ref, bh_ref, bl_ref, out_ref):
        half = NB // 2
        first = pl.program_id(0) == 0
        left_a = (yh_ref[:, pl.ds(0, half)], yl_ref[:, pl.ds(0, half)])
        left_b = (yh_ref[:, pl.ds(half, half)], yl_ref[:, pl.ds(half, half)])
        for b in range(0, group, 2):
            to = (slice(None), pl.ds(b * width, 2 * width))
            parts = []
            for c in (b, b + 1):
                part = sens_ref[pl.ds(c, rows, stride=group), :]
                if c == 0:
                    part = jnp.where(first, own_ref[...], part)
                parts.append(part)
            base = jnp.concatenate(parts, axis=1)
            change = mul3(left_a, (ah_ref[to], al_ref[to]), NN) + mul3(left_b, (bh_ref[to], bl_ref[to]), NN)
            out_ref[to] = base - change

    wide = group * width
    whole = pl.BlockSpec((rows, NB), lambda i: (0, 0))
    part = pl.BlockSpec((NB // 2, wide), lambda i: (0, i))

    def body(sens_ref, *refs):
        kernel(sens_ref.reshape(rows * group, width), *refs)

    return pl.pallas_call(
        body,
        grid=(tiles // group,),
        out_shape=jax.ShapeDtypeStruct((rows, tiles * width), F32),
        in_specs=[
            pl.BlockSpec((rows, group, width), lambda i: (0, i, 0)),
            pl.BlockSpec((rows, width), lambda i: (0, 0)),
            whole,
            whole,
            part,
            part,
            part,
            part,
        ],
        out_specs=pl.BlockSpec((rows, wide), lambda i: (0, i)),
        compiler_params=pltpu.CompilerParams(vmem_limit_bytes=VMEM_BYTES),
        name="trail_first",
    )(sensitivity, own_tile, *solved, *halves)


def trail_second(partial, solved, halves, tiles):
    rows = partial.shape[0]
    width = 128
    group = 8

    def kernel(in_ref, yh_ref, yl_ref, ah_ref, al_ref, bh_ref, bl_ref, out_ref):
        out_ref = out_ref.reshape(rows * group, width)
        half = NB // 2
        left_a = (yh_ref[:, pl.ds(0, half)], yl_ref[:, pl.ds(0, half)])
        left_b = (yh_ref[:, pl.ds(half, half)], yl_ref[:, pl.ds(half, half)])
        for b in range(0, group, 2):
            to = (slice(None), pl.ds(b * width, 2 * width))
            change = mul3(left_a, (ah_ref[to], al_ref[to]), NN) + mul3(left_b, (bh_ref[to], bl_ref[to]), NN)
            value = in_ref[to] - change
            out_ref[pl.ds(b, rows, stride=group), :] = value[:, :width]
            out_ref[pl.ds(b + 1, rows, stride=group), :] = value[:, width:]

    wide = group * width
    whole = pl.BlockSpec((rows, NB), lambda i: (0, 0))
    part = pl.BlockSpec((NB // 2, wide), lambda i: (1, i))
    return pl.pallas_call(
        kernel,
        grid=(tiles // group,),
        out_shape=jax.ShapeDtypeStruct((rows, tiles, width), F32),
        in_specs=[pl.BlockSpec((rows, wide), lambda i: (0, i)), whole, whole, part, part, part, part],
        out_specs=pl.BlockSpec((rows, group, width), lambda i: (0, i, 0)),
        compiler_params=pltpu.CompilerParams(vmem_limit_bytes=VMEM_BYTES),
        name="trail_second",
    )(partial, *solved, *halves)


def place_unknowns(core, parts):
    rows, half = parts[0].shape
    per_step = half // 128
    cycles = 2 * per_step

    def kernel(core_ref, *refs):
        out_ref = refs[-1].reshape(rows * cycles, 128)
        own = pl.program_id(0) == core_ref[0]
        for chosen, wanted in ((refs[0:2], own), (refs[2:4], jnp.logical_not(own))):

            @pl.when(wanted)
            def _(chosen=chosen):
                for step in range(2):
                    for a in range(per_step):
                        out_ref[pl.ds(step * per_step + a, rows, stride=cycles), :] = chosen[step][:, pl.ds(a * 128, 128)]

    spec = pl.BlockSpec((rows, half), lambda i, core_ref: (0, 0))
    return pl.pallas_call(
        kernel,
        out_shape=jax.ShapeDtypeStruct((2 * rows, cycles, 128), F32),
        grid_spec=pltpu.PrefetchScalarGridSpec(
            num_scalar_prefetch=1,
            grid=(2,),
            in_specs=[spec] * 4,
            out_specs=pl.BlockSpec((rows, cycles, 128), lambda i, core_ref: (i, 0, 0)),
        ),
        compiler_params=pltpu.CompilerParams(vmem_limit_bytes=VMEM_BYTES),
        name="place_unknowns",
    )(core, parts[0], parts[2], parts[1], parts[3])


def shards(factor_rows, sensitivity, pivots):
    count = lax.axis_size("pcol")
    sizes = grid_of(count)
    cycles, width, col_tiles = factor_rows.shape[:3]
    rows = sensitivity.shape[0]
    per_block = NB // width
    index = lax.axis_index("pcol")
    core = lax.axis_index("prow")
    tiles = source_tiles(sizes, index)
    swap = lambda value: lax.ppermute(value, "prow", [(0, 1), (1, 0)])

    own_pieces = gather_pieces(sensitivity[:, 0, :], sizes)
    other_rows = swap(factor_rows)
    corner = factor_rows[:, :, 0, :].reshape(cycles * width, width)
    gathered = lax.all_gather(corner, "pcol", axis=0)[: 2 * per_block]
    gathered_other = swap(gathered)

    keep = jnp.stack([index >= per_block, index >= 2 * per_block]).astype(jnp.int32)
    own_halves = prepare(factor_rows, keep, "prepare_own")
    other_halves = prepare(other_rows, keep, "prepare_other")
    halves = (*own_halves, *other_halves)

    wanted = jnp.concatenate([pivots[: 2 * NB], lax.dynamic_slice(pivots, (index * width,), (width,))])
    stripe = permute_columns(own_pieces, sizes, tiles, wanted, rows)
    own_tile = stripe[:, 2 * NB :]

    half = NB // 2
    first_diag, coupling, second_diag = [], [], []
    for side, block in enumerate((gathered, gathered_other)):
        for j in range(per_block):
            first_diag.append((block[j, :half], side * half, j))
            coupling.append((block[per_block + j, :half], side * half, j))
            second_diag.append((block[per_block + j, half:], side * half, j))
    y0, *y0_halves = solve(0, False, (), stripe, [], first_diag)
    partial = trail_first(sensitivity, own_tile, y0_halves, halves)
    y1, *y1_halves = solve(NB, True, y0_halves, stripe, coupling, second_diag)
    updated = trail_second(partial, y1_halves, halves, col_tiles)

    parts = []
    for y in (y0, y1):
        parts += [y[:, :half], swap(y[:, half:])]
    adjoint = place_unknowns(core.reshape(1).astype(jnp.int32), parts)
    return adjoint, updated


def solution(mesh):
    return jax.shard_map(
        shards,
        mesh=mesh,
        in_specs=(P(None, "prow", None, "pcol"), P("prow", None, "pcol"), P()),
        out_specs=(P(None, None, "prow"), P("prow", None, "pcol")),
        check_vma=False,
    )
```

```python
import functools

import jax
import jax.numpy as jnp
from jax import lax
from jax.experimental import pallas as pl
from jax.experimental.pallas import tpu as pltpu
from jax.sharding import PartitionSpec as P

NB = 1024
F32 = jnp.float32
BF16 = jnp.bfloat16
MIB = 1024 * 1024


def grid_of(count):
    z_size = 4
    side = 1
    while side * side * z_size < count:
        side += 1
    return z_size, side, side


def split(value):
    high = value.astype(BF16)
    return high, (value - high.astype(F32)).astype(BF16)


NN = ((1,), (0,))
NT = ((1,), (1,))


def mul3(left, right, dims):
    left = jnp.concatenate([left[0], left[0], left[1]], axis=1)
    right = jnp.concatenate([right[0], right[1], right[0]], axis=dims[1][0])
    return lax.dot_general(left, right, (dims, ((), ())), preferred_element_type=F32)


def gate(wanted, *others):
    return lax.optimization_barrier((wanted, others))[0]


def shift(value, sizes, axis, step):
    z_size, y_size, x_size = sizes
    pairs = []
    for z in range(z_size):
        for y in range(y_size):
            for x in range(x_size):
                at = [z, y, x]
                to = list(at)
                to[axis] = (at[axis] + step) % sizes[axis]
                pairs.append(tuple((c[0] * y_size + c[1]) * x_size + c[2] for c in (at, to)))
    return lax.ppermute(value, "pcol", pairs)


def ring(value, sizes, axis):
    held = [value]
    for _ in range(sizes[axis] - 1):
        held.append(shift(held[-1], sizes, axis, 1))
    return held


def gather_across(layers, sizes):
    half = layers[0].shape[0] // 2
    upper = jnp.concatenate([held[:half] for held in layers], axis=0)
    lower = jnp.concatenate([held[half:] for held in layers], axis=0)
    return jnp.concatenate(ring(upper, sizes, 2), axis=0), jnp.concatenate(ring(lower, sizes, 1), axis=0)


def gather_along(across, sizes):
    return ring(across[0], sizes, 1) + ring(across[1], sizes, 2)


def gathered_places(first_layer, layers, half, sizes):
    places = []
    for dy in range(sizes[1]):
        inner = [((dx * layers + d) * half, 0, (first_layer + d, dy, dx)) for dx in range(sizes[2]) for d in range(layers)]
        places.append(inner)
    for dx in range(sizes[2]):
        inner = [((dy * layers + d) * half, half, (first_layer + d, dy, dx)) for dy in range(sizes[1]) for d in range(layers)]
        places.append(inner)
    return places


def source_tiles(sizes, index):
    z_size, y_size, x_size = sizes
    z, y, x = index // (y_size * x_size), index // x_size % y_size, index % x_size
    places = jnp.arange(z_size * y_size * x_size)
    dz, dy, dx = places // (y_size * x_size), places // x_size % y_size, places % x_size
    return ((z - dz) % z_size * y_size + (y - dy) % y_size) * x_size + (x - dx) % x_size


def slot_of(place, sizes):
    return (place[0] * sizes[1] + place[1]) * sizes[2] + place[2]


def permute_columns(arrays, places, half, sizes, tiles, wanted, rows):
    count = sizes[0] * sizes[1] * sizes[2]
    width = wanted.shape[0]
    step = 256
    depth = count * 128

    def kernel(tiles_ref, wanted_ref, *refs):
        parts, outs, (both_ref, hot_ref) = refs[:-5], refs[-5:-2], refs[-2:]
        for part, inner in zip(parts, places, strict=True):
            for start, first, place in inner:
                high, low = split(part[pl.ds(start, half), :])
                lanes = pl.ds(slot_of(place, sizes) * 128, 128)
                both_ref[pl.ds(first, half), lanes] = high
                both_ref[pl.ds(rows + first, half), lanes] = low
        for start in range(0, width, step):
            size = min(step, width - start)
            columns = wanted_ref[:, pl.ds(start, size)]
            lane = lax.broadcasted_iota(jnp.int32, (128, size), 0)
            for slot in range(count):
                hot = (columns - tiles_ref[slot] * 128) == lane
                hot_ref[pl.ds(slot * 128, 128), pl.ds(0, size)] = hot.astype(F32).astype(BF16)
            got = jnp.dot(both_ref[...], hot_ref[:, pl.ds(0, size)], preferred_element_type=F32)
            outs[start // NB][:, pl.ds(start % NB, size)] = got[:rows] + got[rows:]

    vmem = pl.BlockSpec(memory_space=pltpu.VMEM)
    return pl.pallas_call(
        kernel,
        out_shape=[jax.ShapeDtypeStruct((rows, size), F32) for size in (NB, NB, width - 2 * NB)],
        in_specs=[pl.BlockSpec(memory_space=pltpu.SMEM), vmem] + [vmem] * len(arrays),
        out_specs=[vmem] * 3,
        scratch_shapes=[pltpu.VMEM((2 * rows, depth), BF16), pltpu.VMEM((depth, step), BF16)],
        compiler_params=pltpu.CompilerParams(vmem_limit_bytes=22 * MIB),
        cost_estimate=pl.CostEstimate(flops=4 * rows * depth * width, transcendentals=0, bytes_accessed=8 * rows * depth),
        name="permute_columns",
    )(tiles, wanted.reshape(1, width), *arrays)


def prepare(block, keep, step, name):
    cycles, depth, tiles, width = block.shape
    cycles //= 2

    def kernel(keep_ref, in_ref, high_ref, low_ref):
        own = keep_ref[step]
        for b in range(tiles):
            value = in_ref[0, pl.ds(b, depth, stride=tiles), :]
            if b == 0:
                value = jnp.where(own > 0, value, jnp.zeros_like(value))
            high, low = split(value)
            high_ref[:, pl.ds(b * width, width)] = high
            low_ref[:, pl.ds(b * width, width)] = low

    out = pltpu.HBM((cycles * depth, tiles * width), BF16)
    spec = pl.BlockSpec((depth, tiles * width), lambda a: (a, 0))
    return pl.pallas_call(
        kernel,
        grid=(cycles,),
        out_shape=(out, out),
        in_specs=[
            pl.BlockSpec(memory_space=pltpu.SMEM),
            pl.BlockSpec((1, depth * tiles, width), lambda a: (a + step * cycles, 0, 0)),
        ],
        out_specs=(spec, spec),
        compiler_params=pltpu.CompilerParams(vmem_limit_bytes=12 * MIB),
        cost_estimate=pl.CostEstimate(flops=0, transcendentals=0, bytes_accessed=12 * cycles * depth * tiles * width),
        name=name,
    )(keep, block.reshape(2 * cycles, depth * tiles, width))


def load_blocks(group, tiles_ref, parts, sizes, high_ref, low_ref):
    arrays, places, size, where = group
    half = NB // 2
    at = 0
    for pair, inner in zip(arrays, places, strict=True):
        for side in range(len(pair)):
            part = parts[at]
            if len(part.shape) == 3:
                part = part.reshape(part.shape[0] * part.shape[1], 128)
            at += 1
            for start, first, place in inner:
                belongs, tile, row = where(tiles_ref[slot_of(place, sizes)], first)

                def put(part=part, start=start, tile=tile, row=row, side=side):
                    high, low = split(part[pl.ds(start, size), :])
                    rows_to = pl.ds(pl.multiple_of(row + side * half, 128), size)
                    high_ref[tile, rows_to, :] = high
                    low_ref[tile, rows_to, :] = low

                if sizes[0] * sizes[1] * sizes[2] * 128 <= 2 * NB:
                    put()
                else:
                    pl.when(belongs)(put)


def block_specs(operands, chosen):
    if chosen is None:
        return [pl.BlockSpec(memory_space=pltpu.VMEM)] * len(operands)
    chips, depth, width = operands[0].shape
    spec = pl.BlockSpec((chips, depth // 2, width), lambda i: (0, chosen, 0), pipeline_mode=pl.Buffered(1))
    return [spec] * len(operands)


def solve(tiles, rhs, sizes, diagonal, name, chosen=None):
    rows = rhs.shape[0]
    per_block = NB // 128
    half = NB // 2
    step = 256
    operands = [array for pair in diagonal[0] for array in pair]

    def kernel(tiles_ref, rhs_ref, *refs):
        parts = refs[: len(operands)]
        own_ref, other_ref, out_high, out_low, high_ref, low_ref = refs[len(operands) :]
        load_blocks(diagonal, tiles_ref, parts, sizes, high_ref, low_ref)
        left = split(rhs_ref[...])
        for start in range(0, NB, step):
            wanted = pl.ds(start, step)
            right = tuple(jnp.concatenate([r[t, wanted, :] for t in range(per_block)], axis=1) for r in (high_ref, low_ref))
            value = mul3(left, right, NT)
            out_high[:, wanted], out_low[:, wanted] = split(value)
            to = own_ref if start < half else other_ref
            to[:, pl.ds(start % half, step)] = value

    vmem = pl.BlockSpec(memory_space=pltpu.VMEM)
    f32 = jax.ShapeDtypeStruct((rows, half), F32)
    b16 = jax.ShapeDtypeStruct((rows, NB), BF16)
    return pl.pallas_call(
        kernel,
        out_shape=(f32, f32, b16, b16),
        grid=(1,),
        in_specs=[pl.BlockSpec(memory_space=pltpu.SMEM), vmem, *block_specs(operands, chosen)],
        out_specs=(vmem,) * 4,
        scratch_shapes=[pltpu.VMEM((per_block, NB, 128), BF16)] * 2,
        compiler_params=pltpu.CompilerParams(vmem_limit_bytes=24 * MIB),
        cost_estimate=pl.CostEstimate(flops=6 * rows * NB * NB, transcendentals=0, bytes_accessed=8 * NB * NB),
        name=name,
    )(tiles, rhs, *operands)


def couple(tiles, rhs, sizes, solved, coupling, chosen):
    rows = rhs.shape[0]
    per_block = NB // 128
    operands = [array for pair in coupling[0] for array in pair]

    def kernel(tiles_ref, rhs_ref, yh_ref, yl_ref, *refs):
        parts, (out_ref, high_ref, low_ref) = refs[: len(operands)], refs[len(operands) :]
        load_blocks(coupling, tiles_ref, parts, sizes, high_ref, low_ref)
        left = (yh_ref[...], yl_ref[...])
        for t in range(0, per_block, 2):
            to = (slice(None), pl.ds(t * 128, 256))
            right = tuple(jnp.concatenate([r[t], r[t + 1]], axis=1) for r in (high_ref, low_ref))
            out_ref[to] = rhs_ref[to] - mul3(left, right, NN)

    vmem = pl.BlockSpec(memory_space=pltpu.VMEM)
    return pl.pallas_call(
        kernel,
        out_shape=jax.ShapeDtypeStruct((rows, NB), F32),
        grid=(1,),
        in_specs=[pl.BlockSpec(memory_space=pltpu.SMEM), vmem, vmem, vmem, *block_specs(operands, chosen)],
        out_specs=vmem,
        scratch_shapes=[pltpu.VMEM((per_block, NB, 128), BF16)] * 2,
        compiler_params=pltpu.CompilerParams(vmem_limit_bytes=22 * MIB),
        cost_estimate=pl.CostEstimate(flops=6 * rows * NB * NB, transcendentals=0, bytes_accessed=8 * NB * NB),
        name="couple",
    )(tiles, rhs, *solved, *operands)


def in_hbm(arrays):
    return [pltpu.with_memory_space_constraint(array, pltpu.HBM) for array in arrays]


def trail_specs(rows, wide):
    whole = pl.BlockSpec((rows, NB), lambda i: (0, 0))
    part = pl.BlockSpec((NB // 2, wide), lambda i: (0, i))
    return [whole, whole, part, part, part, part]


def trail_change(refs, to):
    yh_ref, yl_ref, ah_ref, al_ref, bh_ref, bl_ref = refs
    high = jnp.concatenate([ah_ref[to], bh_ref[to]], axis=0)
    low = jnp.concatenate([al_ref[to], bl_ref[to]], axis=0)
    return mul3((yh_ref[...], yl_ref[...]), (high, low), NN)


def trail_cost(rows, tiles):
    return pl.CostEstimate(flops=6 * rows * NB * tiles * 128, transcendentals=0, bytes_accessed=(8 * rows + 4 * NB) * tiles * 128)


def trail_first(sensitivity, own_tile, solved, halves):
    rows, tiles, width = sensitivity.shape
    group = 8

    def kernel(sens_ref, own_ref, *refs):
        refs, out_ref = refs[:-1], refs[-1]
        sens_ref = sens_ref.reshape(rows * group, width)
        first = pl.program_id(0) == 0
        for b in range(0, group, 2):
            to = (slice(None), pl.ds(b * width, 2 * width))
            parts = []
            for c in (b, b + 1):
                part = sens_ref[pl.ds(c, rows, stride=group), :]
                if c == 0:
                    part = jnp.where(first, own_ref[...], part)
                parts.append(part)
            out_ref[to] = jnp.concatenate(parts, axis=1) - trail_change(refs, to)

    wide = group * width
    return pl.pallas_call(
        kernel,
        grid=(tiles // group,),
        out_shape=pltpu.HBM((rows, tiles * width), F32),
        in_specs=[
            pl.BlockSpec((rows, group, width), lambda i: (0, i, 0)),
            pl.BlockSpec((rows, width), lambda i: (0, 0)),
            *trail_specs(rows, wide),
        ],
        out_specs=pl.BlockSpec((rows, wide), lambda i: (0, i)),
        compiler_params=pltpu.CompilerParams(vmem_limit_bytes=24 * MIB),
        cost_estimate=trail_cost(rows, tiles),
        name="trail_first",
    )(*in_hbm([sensitivity]), own_tile, *solved, *in_hbm(halves))


def trail_second(partial, solved, halves, tiles):
    rows = partial.shape[0]
    width = 128
    group = 8

    def kernel(in_ref, *refs):
        refs, out_ref = refs[:-1], refs[-1].reshape(rows * group, width)
        for b in range(0, group, 2):
            to = (slice(None), pl.ds(b * width, 2 * width))
            value = in_ref[to] - trail_change(refs, to)
            out_ref[pl.ds(b, rows, stride=group), :] = value[:, :width]
            out_ref[pl.ds(b + 1, rows, stride=group), :] = value[:, width:]

    wide = group * width
    return pl.pallas_call(
        kernel,
        grid=(tiles // group,),
        out_shape=jax.ShapeDtypeStruct((rows, tiles, width), F32),
        in_specs=[pl.BlockSpec((rows, wide), lambda i: (0, i)), *trail_specs(rows, wide)],
        out_specs=pl.BlockSpec((rows, group, width), lambda i: (0, i, 0)),
        compiler_params=pltpu.CompilerParams(vmem_limit_bytes=24 * MIB),
        cost_estimate=trail_cost(rows, tiles),
        name="trail_second",
    )(*in_hbm([partial]), *solved, *in_hbm(halves))


def place_unknowns(core, parts):
    rows, half = parts[0].shape
    per_step = half // 128
    cycles = 2 * per_step

    def kernel(core_ref, *refs):
        out_ref = refs[-1].reshape(rows * cycles, 128)
        own = pl.program_id(0) == core_ref[0]
        for chosen, wanted in ((refs[0:2], own), (refs[2:4], jnp.logical_not(own))):

            @pl.when(wanted)
            def _(chosen=chosen):
                for step in range(2):
                    for a in range(per_step):
                        out_ref[pl.ds(step * per_step + a, rows, stride=cycles), :] = chosen[step][:, pl.ds(a * 128, 128)]

    spec = pl.BlockSpec((rows, half), lambda i, core_ref: (0, 0))
    return pl.pallas_call(
        kernel,
        out_shape=jax.ShapeDtypeStruct((2 * rows, cycles, 128), F32),
        grid_spec=pltpu.PrefetchScalarGridSpec(
            num_scalar_prefetch=1,
            grid=(2,),
            in_specs=[spec] * 4,
            out_specs=pl.BlockSpec((rows, cycles, 128), lambda i, core_ref: (i, 0, 0)),
        ),
        compiler_params=pltpu.CompilerParams(vmem_limit_bytes=18 * MIB),
        name="place_unknowns",
    )(core, parts[0], parts[2], parts[1], parts[3])


def shards(factor_rows, sensitivity, pivots):
    count = lax.axis_size("pcol")
    sizes = grid_of(count)
    cycles, width, col_tiles = factor_rows.shape[:3]
    rows = sensitivity.shape[0]
    per_block = NB // width
    half = NB // 2
    quarter = half // 2
    index = lax.axis_index("pcol")
    core = lax.axis_index("prow")
    tiles = source_tiles(sizes, index)
    swap = lambda value: lax.ppermute(value, "prow", [(0, 1), (1, 0)])
    step_z = lambda value: shift(value, sizes, 0, 1)
    keep = jnp.stack([index >= per_block, index >= 2 * per_block]).astype(jnp.int32)
    own_columns = lax.dynamic_slice(pivots, (index * width,), (width,))

    stripe_layers = [sensitivity[:, 0, :]]
    corner = factor_rows[:, :, 0, :].reshape(cycles * width, width)
    partners = [(j, j + per_block) for j in range(per_block)] + [(j + per_block, j) for j in range(per_block)]
    shared = jnp.concatenate([corner[quarter:half], corner[half + quarter :]], axis=0)
    received = lax.ppermute(shared, "pcol", partners)
    stripe_layers.append(step_z(stripe_layers[0]))
    other_rows = swap(factor_rows)
    stripe_layers, received, keep = gate((stripe_layers, received, keep))
    first = index < per_block
    diag0 = [jnp.where(first, corner[:quarter], received[:quarter])]
    late = jnp.concatenate(
        [
            jnp.where(first, received[:quarter], corner[:quarter]),
            jnp.where(first, received[quarter:], corner[half : half + quarter]),
        ],
        axis=0,
    )
    late = lax.all_gather(late, "pcol", axis=0)[: 2 * per_block]

    across = gather_across(stripe_layers[:1], sizes)
    stripe_layers.append(step_z(stripe_layers[1]))
    diag0.append(step_z(diag0[0]))
    own0 = prepare(factor_rows, keep, 0, "prepare_own_first")
    stripe_layers, across, keep, diag0 = gate((stripe_layers, across, keep, diag0), own0)

    arrays = [gather_along(across, sizes)]
    across = gather_across(stripe_layers[1:2], sizes)
    stripe_layers.append(step_z(stripe_layers[2]))
    diag0.append(step_z(diag0[1]))
    stripe_layers, across, diag0 = gate((stripe_layers, across, diag0))

    arrays.append(gather_along(across, sizes))
    across = gather_across(stripe_layers[2:3], sizes)
    diag0.append(step_z(diag0[2]))
    across, diag0, keep = gate((across, diag0, keep), arrays[0])

    arrays.append(gather_along(across, sizes))
    across = gather_across(stripe_layers[3:4], sizes)
    across, diag0 = gate((across, diag0), arrays[1])

    arrays.append(gather_along(across, sizes))
    diag_across = gather_across(diag0, sizes)
    other0 = prepare(other_rows, keep, 0, "prepare_other_first")
    diag_across, pivots, keep = gate((diag_across, pivots, keep), arrays, other0)

    diag_arrays = gather_along(diag_across, sizes)
    stripe_places = [p for d in range(sizes[0]) for p in gathered_places(d, 1, rows // 2, sizes)]
    stripe_arrays = [array for layer in arrays for array in layer]
    wanted = jnp.concatenate([pivots[: 2 * NB], own_columns])
    stripe = permute_columns(stripe_arrays, stripe_places, rows // 2, sizes, tiles, wanted, rows)
    rhs0, rhs1, own_tile = stripe
    diag_arrays, keep = gate((diag_arrays, keep), rhs0)
    diag_pairs = [(array, swap(array)) for array in diag_arrays]

    block_places = gathered_places(0, sizes[0], quarter // 2, sizes)
    own1 = prepare(factor_rows, keep, 1, "prepare_own_second")
    other1 = prepare(other_rows, keep, 1, "prepare_other_second")

    def first_rows(tile, row):
        return tile < 2 * per_block, tile % per_block, row + jnp.where(tile < per_block, 0, quarter)

    def second_rows(tile, row):
        return tile < 2 * per_block, tile % per_block, row + jnp.where(tile < per_block, quarter, 0)

    own_y0, other_y0, *y0 = solve(
        tiles, rhs0, sizes, (diag_pairs, block_places, quarter // 2, first_rows), "solve_first"
    )

    late = gate(late, y0, own1, other1)
    late_pairs = [(late, swap(late))]
    late_places = [[(j * quarter, 0, (0, 0, j)) for j in range(2 * per_block)]]
    late_group = (late_pairs, late_places, quarter, second_rows)
    in_order = jnp.arange(2 * per_block)
    partial = trail_first(sensitivity, own_tile, y0, (*own0, *other0))
    rhs1 = couple(in_order, rhs1, sizes, y0, late_group, 0)
    own_y1, other_y1, *y1 = solve(in_order, gate(rhs1, partial), sizes, late_group, "solve_second", 1)
    updated = trail_second(partial, y1, (*own1, *other1), col_tiles)

    parts = [own_y0, swap(other_y0), own_y1, swap(other_y1)]
    adjoint = place_unknowns(core.reshape(1).astype(jnp.int32), parts)
    return adjoint, updated


def solution(mesh):
    return jax.shard_map(
        shards,
        mesh=mesh,
        in_specs=(P(None, "prow", None, "pcol"), P("prow", None, "pcol"), P()),
        out_specs=(P(None, None, "prow"), P("prow", None, "pcol")),
        check_vma=False,
    )
```

```python
import functools

import jax
import jax.numpy as jnp
from jax import lax
from jax.experimental import pallas as pl
from jax.experimental.pallas import tpu as pltpu
from jax.sharding import PartitionSpec as P

NB = 1024
F32 = jnp.float32
BF16 = jnp.bfloat16
MIB = 1024 * 1024


def grid_of(count):
    z_size = 4
    side = 1
    while side * side * z_size < count:
        side += 1
    return z_size, side, side


def split(value):
    high = value.astype(BF16)
    return high, (value - high.astype(F32)).astype(BF16)


NN = ((1,), (0,))
NT = ((1,), (1,))


def mul3(left, right, dims):
    left = jnp.concatenate([left[0], left[0], left[1]], axis=1)
    right = jnp.concatenate([right[0], right[1], right[0]], axis=dims[1][0])
    return lax.dot_general(left, right, (dims, ((), ())), preferred_element_type=F32)


def gate(wanted, *others):
    return lax.optimization_barrier((wanted, others))[0]


def shift(value, sizes, axis, step):
    z_size, y_size, x_size = sizes
    pairs = []
    for z in range(z_size):
        for y in range(y_size):
            for x in range(x_size):
                at = [z, y, x]
                to = list(at)
                to[axis] = (at[axis] + step) % sizes[axis]
                pairs.append(tuple((c[0] * y_size + c[1]) * x_size + c[2] for c in (at, to)))
    return lax.ppermute(value, "pcol", pairs)


def ring(value, sizes, axis):
    held = [value]
    for _ in range(sizes[axis] - 1):
        held.append(shift(held[-1], sizes, axis, 1))
    return held


def gather_across(layers, sizes):
    half = layers[0].shape[0] // 2
    upper = jnp.concatenate([held[:half] for held in layers], axis=0)
    lower = jnp.concatenate([held[half:] for held in layers], axis=0)
    return jnp.concatenate(ring(upper, sizes, 2), axis=0), jnp.concatenate(ring(lower, sizes, 1), axis=0)


def gather_along(across, sizes):
    return ring(across[0], sizes, 1) + ring(across[1], sizes, 2)


def gathered_places(first_layer, layers, half, sizes):
    places = []
    for dy in range(sizes[1]):
        inner = [((dx * layers + d) * half, 0, (first_layer + d, dy, dx)) for dx in range(sizes[2]) for d in range(layers)]
        places.append(inner)
    for dx in range(sizes[2]):
        inner = [((dy * layers + d) * half, half, (first_layer + d, dy, dx)) for dy in range(sizes[1]) for d in range(layers)]
        places.append(inner)
    return places


def end_to_end(arrays, places):
    inner, base = [], 0
    for array, own in zip(arrays, places, strict=True):
        inner += [(base + start, first, place) for start, first, place in own]
        base += array.shape[0]
    return jnp.concatenate(arrays, axis=0), inner


def source_tiles(sizes, index):
    z_size, y_size, x_size = sizes
    z, y, x = index // (y_size * x_size), index // x_size % y_size, index % x_size
    places = jnp.arange(z_size * y_size * x_size)
    dz, dy, dx = places // (y_size * x_size), places // x_size % y_size, places % x_size
    return ((z - dz) % z_size * y_size + (y - dy) % y_size) * x_size + (x - dx) % x_size


def slot_of(place, sizes):
    return (place[0] * sizes[1] + place[1]) * sizes[2] + place[2]


def permute_columns(arrays, places, half, sizes, tiles, wanted, rows):
    count = sizes[0] * sizes[1] * sizes[2]
    width = wanted.shape[0]
    step = 256
    depth = count * 128

    def kernel(tiles_ref, wanted_ref, *refs):
        parts, outs, (both_ref, hot_ref) = refs[:-5], refs[-5:-2], refs[-2:]
        for part, inner in zip(parts, places, strict=True):
            for start, first, place in inner:
                high, low = split(part[pl.ds(start, half), :])
                lanes = pl.ds(slot_of(place, sizes) * 128, 128)
                both_ref[pl.ds(first, half), lanes] = high
                both_ref[pl.ds(rows + first, half), lanes] = low
        def pick(start, size, out_ref, to):
            columns = wanted_ref[:, pl.ds(start, size)]
            lane = lax.broadcasted_iota(jnp.int32, (128, size), 0)
            for slot in range(count):
                hot = (columns - tiles_ref[slot] * 128) == lane
                hot_ref[pl.ds(slot * 128, 128), pl.ds(0, size)] = hot.astype(F32).astype(BF16)
            got = jnp.dot(both_ref[...], hot_ref[:, pl.ds(0, size)], preferred_element_type=F32)
            out_ref[:, pl.ds(to, size)] = got[:rows] + got[rows:]

        for k in range(2):

            @pl.loop(0, NB // step, unroll=NB // step if depth <= 2 * NB else 1)
            def _(i, k=k):
                to = pl.multiple_of(i * step, step)
                pick(k * NB + to, step, outs[k], to)

        pick(2 * NB, width - 2 * NB, outs[2], 0)

    vmem = pl.BlockSpec(memory_space=pltpu.VMEM)
    return pl.pallas_call(
        kernel,
        out_shape=[jax.ShapeDtypeStruct((rows, size), F32) for size in (NB, NB, width - 2 * NB)],
        in_specs=[pl.BlockSpec(memory_space=pltpu.SMEM), vmem] + [vmem] * len(arrays),
        out_specs=[vmem] * 3,
        scratch_shapes=[pltpu.VMEM((2 * rows, depth), BF16), pltpu.VMEM((depth, step), BF16)],
        compiler_params=pltpu.CompilerParams(vmem_limit_bytes=22 * MIB),
        cost_estimate=pl.CostEstimate(flops=4 * rows * depth * width, transcendentals=0, bytes_accessed=8 * rows * depth),
        name="permute_columns",
    )(tiles, wanted.reshape(1, width), *arrays)


def in_hbm(arrays):
    return [pltpu.with_memory_space_constraint(array, pltpu.HBM) for array in arrays]


def prepare(block, keep, step, name):
    cycles, depth, tiles, width = block.shape
    cycles //= 2

    def kernel(keep_ref, in_ref, high_ref, low_ref):
        own = keep_ref[step]
        for b in range(tiles):
            value = in_ref[0, pl.ds(b, depth, stride=tiles), :]
            if b == 0:
                value = jnp.where(own > 0, value, jnp.zeros_like(value))
            high, low = split(value)
            high_ref[:, pl.ds(b * width, width)] = high
            low_ref[:, pl.ds(b * width, width)] = low

    out = pltpu.HBM((cycles * depth, tiles * width), BF16)
    spec = pl.BlockSpec((depth, tiles * width), lambda a: (a, 0))
    return pl.pallas_call(
        kernel,
        grid=(cycles,),
        out_shape=(out, out),
        in_specs=[
            pl.BlockSpec(memory_space=pltpu.SMEM),
            pl.BlockSpec((1, depth * tiles, width), lambda a: (a + step * cycles, 0, 0)),
        ],
        out_specs=(spec, spec),
        compiler_params=pltpu.CompilerParams(vmem_limit_bytes=12 * MIB),
        cost_estimate=pl.CostEstimate(flops=0, transcendentals=0, bytes_accessed=12 * cycles * depth * tiles * width),
        name=name,
    )(keep, *in_hbm([block.reshape(2 * cycles, depth * tiles, width)]))


def load_blocks(group, tiles_ref, parts, sizes, high_ref, low_ref):
    arrays, places, size, where = group
    half = NB // 2
    at = 0
    for pair, inner in zip(arrays, places, strict=True):
        for side in range(len(pair)):
            part = parts[at]
            if len(part.shape) == 3:
                part = part.reshape(part.shape[0] * part.shape[1], 128)
            at += 1
            for start, first, place in inner:
                belongs, tile, row = where(tiles_ref[slot_of(place, sizes)], first)

                def put(part=part, start=start, tile=tile, row=row, side=side):
                    high, low = split(part[pl.ds(start, size), :])
                    rows_to = pl.ds(pl.multiple_of(row + side * half, 128), size)
                    high_ref[tile, rows_to, :] = high
                    low_ref[tile, rows_to, :] = low

                if sizes[0] * sizes[1] * sizes[2] * 128 <= 2 * NB:
                    put()
                else:
                    pl.when(belongs)(put)


def block_specs(operands, chosen):
    if chosen is None:
        return [pl.BlockSpec(memory_space=pltpu.VMEM)] * len(operands)
    chips, depth, width = operands[0].shape
    spec = pl.BlockSpec((chips, depth // 2, width), lambda i: (0, chosen, 0), pipeline_mode=pl.Buffered(1))
    return [spec] * len(operands)


def solve(tiles, rhs, sizes, diagonal, name, chosen=None):
    rows = rhs.shape[0]
    per_block = NB // 128
    half = NB // 2
    step = 256
    operands = [array for pair in diagonal[0] for array in pair]

    def kernel(tiles_ref, rhs_ref, *refs):
        parts = refs[: len(operands)]
        own_ref, other_ref, out_high, out_low, high_ref, low_ref = refs[len(operands) :]
        load_blocks(diagonal, tiles_ref, parts, sizes, high_ref, low_ref)
        left = split(rhs_ref[...])
        for start in range(0, NB, step):
            wanted = pl.ds(start, step)
            right = tuple(jnp.concatenate([r[t, wanted, :] for t in range(per_block)], axis=1) for r in (high_ref, low_ref))
            value = mul3(left, right, NT)
            out_high[:, wanted], out_low[:, wanted] = split(value)
            to = own_ref if start < half else other_ref
            to[:, pl.ds(start % half, step)] = value

    vmem = pl.BlockSpec(memory_space=pltpu.VMEM)
    f32 = jax.ShapeDtypeStruct((rows, half), F32)
    b16 = pltpu.HBM((rows, NB), BF16)
    whole = pl.BlockSpec((rows, NB), lambda i: (0, 0), pipeline_mode=pl.Buffered(1))
    return pl.pallas_call(
        kernel,
        out_shape=(f32, f32, b16, b16),
        grid=(1,),
        in_specs=[pl.BlockSpec(memory_space=pltpu.SMEM), vmem, *block_specs(operands, chosen)],
        out_specs=(vmem, vmem, whole, whole),
        scratch_shapes=[pltpu.VMEM((per_block, NB, 128), BF16)] * 2,
        compiler_params=pltpu.CompilerParams(vmem_limit_bytes=24 * MIB),
        cost_estimate=pl.CostEstimate(flops=6 * rows * NB * NB, transcendentals=0, bytes_accessed=8 * NB * NB),
        name=name,
    )(tiles, rhs, *operands)


def couple(tiles, rhs, sizes, solved, coupling, chosen):
    rows = rhs.shape[0]
    per_block = NB // 128
    operands = [array for pair in coupling[0] for array in pair]

    def kernel(tiles_ref, rhs_ref, yh_ref, yl_ref, *refs):
        parts, (out_ref, high_ref, low_ref) = refs[: len(operands)], refs[len(operands) :]
        load_blocks(coupling, tiles_ref, parts, sizes, high_ref, low_ref)
        left = (yh_ref[...], yl_ref[...])
        for t in range(0, per_block, 2):
            to = (slice(None), pl.ds(t * 128, 256))
            right = tuple(jnp.concatenate([r[t], r[t + 1]], axis=1) for r in (high_ref, low_ref))
            out_ref[to] = rhs_ref[to] - mul3(left, right, NN)

    vmem = pl.BlockSpec(memory_space=pltpu.VMEM)
    whole = pl.BlockSpec((rows, NB), lambda i: (0, 0), pipeline_mode=pl.Buffered(1))
    return pl.pallas_call(
        kernel,
        out_shape=jax.ShapeDtypeStruct((rows, NB), F32),
        grid=(1,),
        in_specs=[pl.BlockSpec(memory_space=pltpu.SMEM), vmem, whole, whole, *block_specs(operands, chosen)],
        out_specs=vmem,
        scratch_shapes=[pltpu.VMEM((per_block, NB, 128), BF16)] * 2,
        compiler_params=pltpu.CompilerParams(vmem_limit_bytes=22 * MIB),
        cost_estimate=pl.CostEstimate(flops=6 * rows * NB * NB, transcendentals=0, bytes_accessed=8 * NB * NB),
        name="couple",
    )(tiles, rhs, *in_hbm(solved), *operands)


def trail_specs(rows, wide):
    whole = pl.BlockSpec((rows, NB), lambda i: (0, 0), pipeline_mode=pl.Buffered(1))
    part = pl.BlockSpec((NB // 2, wide), lambda i: (0, i))
    return [whole, whole, part, part, part, part]


def trail_change(refs, to):
    yh_ref, yl_ref, ah_ref, al_ref, bh_ref, bl_ref = refs
    high = jnp.concatenate([ah_ref[to], bh_ref[to]], axis=0)
    low = jnp.concatenate([al_ref[to], bl_ref[to]], axis=0)
    return mul3((yh_ref[...], yl_ref[...]), (high, low), NN)


def trail_cost(rows, tiles):
    return pl.CostEstimate(flops=6 * rows * NB * tiles * 128, transcendentals=0, bytes_accessed=(8 * rows + 4 * NB) * tiles * 128)


def trail_first(sensitivity, own_tile, solved, halves):
    rows, tiles, width = sensitivity.shape
    group = 8

    def kernel(sens_ref, own_ref, *refs):
        refs, out_ref = refs[:-1], refs[-1]
        sens_ref = sens_ref.reshape(rows * group, width)
        first = pl.program_id(0) == 0
        for b in range(0, group, 2):
            to = (slice(None), pl.ds(b * width, 2 * width))
            parts = []
            for c in (b, b + 1):
                part = sens_ref[pl.ds(c, rows, stride=group), :]
                if c == 0:
                    part = jnp.where(first, own_ref[...], part)
                parts.append(part)
            out_ref[to] = jnp.concatenate(parts, axis=1) - trail_change(refs, to)

    wide = group * width
    return pl.pallas_call(
        kernel,
        grid=(tiles // group,),
        out_shape=pltpu.HBM((rows, tiles * width), F32),
        in_specs=[
            pl.BlockSpec((rows, group, width), lambda i: (0, i, 0)),
            pl.BlockSpec((rows, width), lambda i: (0, 0)),
            *trail_specs(rows, wide),
        ],
        out_specs=pl.BlockSpec((rows, wide), lambda i: (0, i)),
        compiler_params=pltpu.CompilerParams(vmem_limit_bytes=24 * MIB),
        cost_estimate=trail_cost(rows, tiles),
        name="trail_first",
    )(*in_hbm([sensitivity]), own_tile, *in_hbm([*solved, *halves]))


def trail_second(partial, solved, halves, tiles):
    rows = partial.shape[0]
    width = 128
    group = 8

    def kernel(in_ref, *refs):
        refs, out_ref = refs[:-1], refs[-1].reshape(rows * group, width)
        for b in range(0, group, 2):
            to = (slice(None), pl.ds(b * width, 2 * width))
            value = in_ref[to] - trail_change(refs, to)
            out_ref[pl.ds(b, rows, stride=group), :] = value[:, :width]
            out_ref[pl.ds(b + 1, rows, stride=group), :] = value[:, width:]

    wide = group * width
    return pl.pallas_call(
        kernel,
        grid=(tiles // group,),
        out_shape=jax.ShapeDtypeStruct((rows, tiles, width), F32),
        in_specs=[pl.BlockSpec((rows, wide), lambda i: (0, i)), *trail_specs(rows, wide)],
        out_specs=pl.BlockSpec((rows, group, width), lambda i: (0, i, 0)),
        compiler_params=pltpu.CompilerParams(vmem_limit_bytes=24 * MIB),
        cost_estimate=trail_cost(rows, tiles),
        name="trail_second",
    )(*in_hbm([partial, *solved, *halves]))


def place_unknowns(core, parts):
    rows, half = parts[0].shape
    per_step = half // 128
    cycles = 2 * per_step

    def kernel(core_ref, *refs):
        out_ref = refs[-1].reshape(rows * cycles, 128)
        own = pl.program_id(0) == core_ref[0]
        for chosen, wanted in ((refs[0:2], own), (refs[2:4], jnp.logical_not(own))):

            @pl.when(wanted)
            def _(chosen=chosen):
                for step in range(2):
                    for a in range(per_step):
                        out_ref[pl.ds(step * per_step + a, rows, stride=cycles), :] = chosen[step][:, pl.ds(a * 128, 128)]

    spec = pl.BlockSpec((rows, half), lambda i, core_ref: (0, 0))
    return pl.pallas_call(
        kernel,
        out_shape=jax.ShapeDtypeStruct((2 * rows, cycles, 128), F32),
        grid_spec=pltpu.PrefetchScalarGridSpec(
            num_scalar_prefetch=1,
            grid=(2,),
            in_specs=[spec] * 4,
            out_specs=pl.BlockSpec((rows, cycles, 128), lambda i, core_ref: (i, 0, 0)),
        ),
        compiler_params=pltpu.CompilerParams(vmem_limit_bytes=18 * MIB),
        name="place_unknowns",
    )(core, parts[0], parts[2], parts[1], parts[3])


def shards(factor_rows, sensitivity, pivots):
    count = lax.axis_size("pcol")
    sizes = grid_of(count)
    cycles, width, col_tiles = factor_rows.shape[:3]
    rows = sensitivity.shape[0]
    per_block = NB // width
    half = NB // 2
    quarter = half // 2
    index = lax.axis_index("pcol")
    core = lax.axis_index("prow")
    tiles = source_tiles(sizes, index)
    swap = lambda value: lax.ppermute(value, "prow", [(0, 1), (1, 0)])
    step_z = lambda value: shift(value, sizes, 0, 1)
    keep = jnp.stack([index >= per_block, index >= 2 * per_block]).astype(jnp.int32)
    own_columns = lax.dynamic_slice(pivots, (index * width,), (width,))

    stripe_layers = [lax.optimization_barrier(sensitivity[:, 0, :])]
    stripe_layers.append(step_z(stripe_layers[0]))
    corner = factor_rows[:, :, 0, :].reshape(cycles * width, width)
    partners = [(j, j + per_block) for j in range(per_block)] + [(j + per_block, j) for j in range(per_block)]
    shared = jnp.concatenate([corner[quarter:half], corner[half + quarter :]], axis=0)
    received = lax.ppermute(shared, "pcol", partners)
    other_rows = swap(factor_rows)
    across = gather_across(stripe_layers[:1], sizes)
    own0 = prepare(factor_rows, keep, 0, "prepare_own_first")
    first = index < per_block
    diag0 = [jnp.where(first, corner[:quarter], received[:quarter])]
    late = [
        jnp.concatenate(
            [
                jnp.where(first, received[:quarter], corner[:quarter]),
                jnp.where(first, received[quarter:], corner[half : half + quarter]),
            ],
            axis=0,
        )
    ]
    stripe_layers[1], across, keep, diag0[0], late[0] = gate((stripe_layers[1], across, keep, diag0[0], late[0]), own0)

    stripe_layers.append(step_z(stripe_layers[1]))
    arrays = [gather_along(across, sizes)]
    diag0.append(step_z(diag0[0]))
    across = gather_across(stripe_layers[1:2], sizes)
    own1 = prepare(factor_rows, keep, 1, "prepare_own_second")
    stripe_layers[2], across, keep, diag0[1], late[0] = gate((stripe_layers[2], across, keep, diag0[1], late[0]), own1)

    stripe_layers.append(step_z(stripe_layers[2]))
    arrays.append(gather_along(across, sizes))
    diag0.append(step_z(diag0[1]))
    across = gather_across(stripe_layers[2:3], sizes)
    late.append(step_z(late[0]))
    stripe_layers[3], across, keep, diag0[2], late[1] = gate(
        (stripe_layers[3], across, keep, diag0[2], late[1]), arrays[0]
    )

    arrays.append(gather_along(across, sizes))
    across = gather_across(stripe_layers[3:4], sizes)
    diag0.append(step_z(diag0[2]))
    late.append(step_z(late[1]))
    other0 = prepare(other_rows, keep, 0, "prepare_other_first")
    across, keep, diag0[3], late[2] = gate((across, keep, diag0[3], late[2]), arrays[1], other0)

    arrays.append(gather_along(across, sizes))
    late.append(step_z(late[2]))
    diag_across = gather_across(diag0, sizes)
    other1 = prepare(other_rows, keep, 1, "prepare_other_second")
    diag_across, late[3], pivots = gate((diag_across, late[3], pivots), arrays, other1)

    diag_arrays = gather_along(diag_across, sizes)
    late_across = gather_across(late, sizes)
    stripe_places = [p for d in range(sizes[0]) for p in gathered_places(d, 1, rows // 2, sizes)]
    stripe_arrays = [array for layer in arrays for array in layer]
    wanted = jnp.concatenate([pivots[: 2 * NB], own_columns])
    rhs0, rhs1, own_tile = permute_columns(stripe_arrays, stripe_places, rows // 2, sizes, tiles, wanted, rows)
    late_across, diag_arrays = gate((late_across, diag_arrays), rhs0)

    late_arrays = gather_along(late_across, sizes)
    own_diag, diag_places = end_to_end(diag_arrays, gathered_places(0, sizes[0], quarter // 2, sizes))

    def first_rows(tile, row):
        return tile < 2 * per_block, tile % per_block, row + jnp.where(tile < per_block, 0, quarter)

    def second_rows(tile, row):
        return tile < 2 * per_block, tile % per_block, row + jnp.where(tile < per_block, quarter, 0)

    own_y0, other_y0, *y0 = solve(
        tiles, rhs0, sizes, ([(own_diag, swap(own_diag))], [diag_places], quarter // 2, first_rows), "solve_first"
    )
    partial = trail_first(sensitivity, own_tile, y0, (*own0, *other0))
    swapped_y0 = swap(other_y0)

    ups = sizes[1]
    held = (0, ups)
    early = {k: swap(late_arrays[k]) for k in held}
    late_arrays, early, rhs1, swapped_y0 = gate((late_arrays, early, rhs1, swapped_y0), partial)
    pairs = [(array, early[k] if k in held else swap(array)) for k, array in enumerate(late_arrays)]
    late_places = gathered_places(0, sizes[0], quarter, sizes)
    couple_group = (pairs[:ups], late_places[:ups], quarter, second_rows)
    second_group = (
        pairs[ups:],
        [[(start, row - quarter, place) for start, row, place in inner] for inner in late_places[ups:]],
        quarter,
        second_rows,
    )
    rhs1 = couple(tiles, rhs1, sizes, y0, couple_group, None)
    own_y1, other_y1, *y1 = solve(tiles, rhs1, sizes, second_group, "solve_second")
    updated = trail_second(partial, y1, (*own1, *other1), col_tiles)

    adjoint = place_unknowns(core.reshape(1).astype(jnp.int32), [own_y0, swapped_y0, own_y1, swap(other_y1)])
    return adjoint, updated


def solution(mesh):
    return jax.shard_map(
        shards,
        mesh=mesh,
        in_specs=(P(None, "prow", None, "pcol"), P("prow", None, "pcol"), P()),
        out_specs=(P(None, None, "prow"), P("prow", None, "pcol")),
        check_vma=False,
    )
```

```python
import functools

import jax
import jax.numpy as jnp
from jax import lax
from jax.experimental import pallas as pl
from jax.experimental.pallas import tpu as pltpu
from jax.sharding import PartitionSpec as P

NB = 1024
F32 = jnp.float32
BF16 = jnp.bfloat16
MIB = 1024 * 1024


def grid_of(count):
    z_size = 4
    side = 1
    while side * side * z_size < count:
        side += 1
    return z_size, side, side


def split(value):
    high = value.astype(BF16)
    return high, (value - high.astype(F32)).astype(BF16)


NN = ((1,), (0,))
NT = ((1,), (1,))


def mul3(left, right, dims):
    left = jnp.concatenate([left[0], left[0], left[1]], axis=1)
    right = jnp.concatenate([right[0], right[1], right[0]], axis=dims[1][0])
    return lax.dot_general(left, right, (dims, ((), ())), preferred_element_type=F32)


def gate(wanted, *others):
    return lax.optimization_barrier((wanted, others))[0]


def shift(value, sizes, axis, step):
    z_size, y_size, x_size = sizes
    pairs = []
    for z in range(z_size):
        for y in range(y_size):
            for x in range(x_size):
                at = [z, y, x]
                to = list(at)
                to[axis] = (at[axis] + step) % sizes[axis]
                pairs.append(tuple((c[0] * y_size + c[1]) * x_size + c[2] for c in (at, to)))
    return lax.ppermute(value, "pcol", pairs)


def ring(value, sizes, axis):
    held = [value]
    for _ in range(sizes[axis] - 1):
        held.append(shift(held[-1], sizes, axis, 1))
    return held


def gather_across(layers, sizes):
    half = layers[0].shape[0] // 2
    upper = jnp.concatenate([held[:half] for held in layers], axis=0)
    lower = jnp.concatenate([held[half:] for held in layers], axis=0)
    return jnp.concatenate(ring(upper, sizes, 2), axis=0), jnp.concatenate(ring(lower, sizes, 1), axis=0)


def gather_along(across, sizes):
    return ring(across[0], sizes, 1) + ring(across[1], sizes, 2)


def gathered_places(first_layer, layers, half, sizes):
    places = []
    for dy in range(sizes[1]):
        inner = [((dx * layers + d) * half, 0, (first_layer + d, dy, dx)) for dx in range(sizes[2]) for d in range(layers)]
        places.append(inner)
    for dx in range(sizes[2]):
        inner = [((dy * layers + d) * half, half, (first_layer + d, dy, dx)) for dy in range(sizes[1]) for d in range(layers)]
        places.append(inner)
    return places


def end_to_end(arrays, places):
    inner, base = [], 0
    for array, own in zip(arrays, places, strict=True):
        inner += [(base + start, first, place) for start, first, place in own]
        base += array.shape[0]
    return jnp.concatenate(arrays, axis=0), inner


def source_tiles(sizes, index):
    z_size, y_size, x_size = sizes
    z, y, x = index // (y_size * x_size), index // x_size % y_size, index % x_size
    places = jnp.arange(z_size * y_size * x_size)
    dz, dy, dx = places // (y_size * x_size), places // x_size % y_size, places % x_size
    return ((z - dz) % z_size * y_size + (y - dy) % y_size) * x_size + (x - dx) % x_size


def slot_of(place, sizes):
    return (place[0] * sizes[1] + place[1]) * sizes[2] + place[2]


def permute_columns(arrays, places, half, sizes, tiles, wanted, rows):
    count = sizes[0] * sizes[1] * sizes[2]
    width = wanted.shape[0]
    step = 256
    depth = count * 128

    def kernel(tiles_ref, wanted_ref, *refs):
        parts, outs, (both_ref, hot_ref) = refs[:-5], refs[-5:-2], refs[-2:]
        for part, inner in zip(parts, places, strict=True):
            for start, first, place in inner:
                high, low = split(part[pl.ds(start, half), :])
                lanes = pl.ds(slot_of(place, sizes) * 128, 128)
                both_ref[pl.ds(first, half), lanes] = high
                both_ref[pl.ds(rows + first, half), lanes] = low
        def pick(start, size, out_ref, to):
            columns = wanted_ref[:, pl.ds(start, size)]
            lane = lax.broadcasted_iota(jnp.int32, (128, size), 0)
            for slot in range(count):
                hot = (columns - tiles_ref[slot] * 128) == lane
                hot_ref[pl.ds(slot * 128, 128), pl.ds(0, size)] = hot.astype(F32).astype(BF16)
            got = jnp.dot(both_ref[...], hot_ref[:, pl.ds(0, size)], preferred_element_type=F32)
            out_ref[:, pl.ds(to, size)] = got[:rows] + got[rows:]

        for k in range(2):

            @pl.loop(0, NB // step, unroll=NB // step if depth <= 2 * NB else 1)
            def _(i, k=k):
                to = pl.multiple_of(i * step, step)
                pick(k * NB + to, step, outs[k], to)

        pick(2 * NB, width - 2 * NB, outs[2], 0)

    vmem = pl.BlockSpec(memory_space=pltpu.VMEM)
    return pl.pallas_call(
        kernel,
        out_shape=[jax.ShapeDtypeStruct((rows, size), F32) for size in (NB, NB, width - 2 * NB)],
        in_specs=[pl.BlockSpec(memory_space=pltpu.SMEM), vmem] + [vmem] * len(arrays),
        out_specs=[vmem] * 3,
        scratch_shapes=[pltpu.VMEM((2 * rows, depth), BF16), pltpu.VMEM((depth, step), BF16)],
        compiler_params=pltpu.CompilerParams(vmem_limit_bytes=22 * MIB),
        cost_estimate=pl.CostEstimate(flops=4 * rows * depth * width, transcendentals=0, bytes_accessed=8 * rows * depth),
        name="permute_columns",
    )(tiles, wanted.reshape(1, width), *arrays)


def in_hbm(arrays):
    return [pltpu.with_memory_space_constraint(array, pltpu.HBM) for array in arrays]


def prepare(block, keep, step, name):
    cycles, depth, tiles, width = block.shape
    cycles //= 2

    def kernel(keep_ref, in_ref, high_ref, low_ref):
        own = keep_ref[step]
        for b in range(tiles):
            value = in_ref[0, pl.ds(b, depth, stride=tiles), :]
            if b == 0:
                value = jnp.where(own > 0, value, jnp.zeros_like(value))
            high, low = split(value)
            high_ref[:, pl.ds(b * width, width)] = high
            low_ref[:, pl.ds(b * width, width)] = low

    out = pltpu.HBM((cycles * depth, tiles * width), BF16)
    spec = pl.BlockSpec((depth, tiles * width), lambda a: (a, 0))
    return pl.pallas_call(
        kernel,
        grid=(cycles,),
        out_shape=(out, out),
        in_specs=[
            pl.BlockSpec(memory_space=pltpu.SMEM),
            pl.BlockSpec((1, depth * tiles, width), lambda a: (a + step * cycles, 0, 0)),
        ],
        out_specs=(spec, spec),
        compiler_params=pltpu.CompilerParams(vmem_limit_bytes=12 * MIB),
        cost_estimate=pl.CostEstimate(flops=0, transcendentals=0, bytes_accessed=12 * cycles * depth * tiles * width),
        name=name,
    )(keep, *in_hbm([block.reshape(2 * cycles, depth * tiles, width)]))


def load_blocks(group, tiles_ref, parts, sizes, high_ref, low_ref):
    arrays, places, size, where = group
    half = NB // 2
    at = 0
    for pair, inner in zip(arrays, places, strict=True):
        for side in range(len(pair)):
            part = parts[at]
            if len(part.shape) == 3:
                part = part.reshape(part.shape[0] * part.shape[1], 128)
            at += 1
            for start, first, place in inner:
                belongs, tile, row = where(tiles_ref[slot_of(place, sizes)], first)

                def put(part=part, start=start, tile=tile, row=row, side=side):
                    high, low = split(part[pl.ds(start, size), :])
                    rows_to = pl.ds(pl.multiple_of(row + side * half, 128), size)
                    high_ref[tile, rows_to, :] = high
                    low_ref[tile, rows_to, :] = low

                if sizes[0] * sizes[1] * sizes[2] * 128 <= 2 * NB:
                    put()
                else:
                    pl.when(belongs)(put)


def block_specs(operands, chosen):
    if chosen is None:
        return [pl.BlockSpec(memory_space=pltpu.VMEM)] * len(operands)
    chips, depth, width = operands[0].shape
    spec = pl.BlockSpec((chips, depth // 2, width), lambda i: (0, chosen, 0), pipeline_mode=pl.Buffered(1))
    return [spec] * len(operands)


def solve(tiles, rhs, sizes, diagonal, name, chosen=None, to_hbm=False):
    rows = rhs.shape[0]
    per_block = NB // 128
    half = NB // 2
    step = 256
    operands = [array for pair in diagonal[0] for array in pair]

    def kernel(tiles_ref, rhs_ref, *refs):
        parts = refs[: len(operands)]
        own_ref, other_ref, out_high, out_low, high_ref, low_ref = refs[len(operands) :]
        load_blocks(diagonal, tiles_ref, parts, sizes, high_ref, low_ref)
        left = split(rhs_ref[...])
        for start in range(0, NB, step):
            wanted = pl.ds(start, step)
            right = tuple(jnp.concatenate([r[t, wanted, :] for t in range(per_block)], axis=1) for r in (high_ref, low_ref))
            value = mul3(left, right, NT)
            out_high[:, wanted], out_low[:, wanted] = split(value)
            to = own_ref if start < half else other_ref
            to[:, pl.ds(start % half, step)] = value

    vmem = pl.BlockSpec(memory_space=pltpu.VMEM)
    f32 = jax.ShapeDtypeStruct((rows, half), F32)
    b16 = jax.ShapeDtypeStruct((rows, NB), BF16)
    halves_spec = vmem
    if to_hbm:
        b16 = pltpu.HBM((rows, NB), BF16)
        halves_spec = pl.BlockSpec((rows, NB), lambda i: (0, 0), pipeline_mode=pl.Buffered(1))
    return pl.pallas_call(
        kernel,
        out_shape=(f32, f32, b16, b16),
        grid=(1,),
        in_specs=[pl.BlockSpec(memory_space=pltpu.SMEM), vmem, *block_specs(operands, chosen)],
        out_specs=(vmem, vmem, halves_spec, halves_spec),
        scratch_shapes=[pltpu.VMEM((per_block, NB, 128), BF16)] * 2,
        compiler_params=pltpu.CompilerParams(vmem_limit_bytes=24 * MIB),
        cost_estimate=pl.CostEstimate(flops=6 * rows * NB * NB, transcendentals=0, bytes_accessed=8 * NB * NB),
        name=name,
    )(tiles, rhs, *operands)


def couple(tiles, rhs, sizes, solved, coupling, chosen):
    rows = rhs.shape[0]
    per_block = NB // 128
    operands = [array for pair in coupling[0] for array in pair]

    def kernel(tiles_ref, rhs_ref, yh_ref, yl_ref, *refs):
        parts, (out_ref, high_ref, low_ref) = refs[: len(operands)], refs[len(operands) :]
        load_blocks(coupling, tiles_ref, parts, sizes, high_ref, low_ref)
        left = (yh_ref[...], yl_ref[...])
        for t in range(0, per_block, 2):
            to = (slice(None), pl.ds(t * 128, 256))
            right = tuple(jnp.concatenate([r[t], r[t + 1]], axis=1) for r in (high_ref, low_ref))
            out_ref[to] = rhs_ref[to] - mul3(left, right, NN)

    vmem = pl.BlockSpec(memory_space=pltpu.VMEM)
    return pl.pallas_call(
        kernel,
        out_shape=jax.ShapeDtypeStruct((rows, NB), F32),
        grid=(1,),
        in_specs=[pl.BlockSpec(memory_space=pltpu.SMEM), vmem, vmem, vmem, *block_specs(operands, chosen)],
        out_specs=vmem,
        scratch_shapes=[pltpu.VMEM((per_block, NB, 128), BF16)] * 2,
        compiler_params=pltpu.CompilerParams(vmem_limit_bytes=22 * MIB),
        cost_estimate=pl.CostEstimate(flops=6 * rows * NB * NB, transcendentals=0, bytes_accessed=8 * NB * NB),
        name="couple",
    )(tiles, rhs, *solved, *operands)


def trail_specs(rows, wide, in_vmem):
    whole = pl.BlockSpec((rows, NB), lambda i: (0, 0), pipeline_mode=pl.Buffered(1))
    if in_vmem:
        whole = pl.BlockSpec(memory_space=pltpu.VMEM)
    part = pl.BlockSpec((NB // 2, wide), lambda i: (0, i))
    return [whole, whole, part, part, part, part]


def trail_change(refs, to):
    yh_ref, yl_ref, ah_ref, al_ref, bh_ref, bl_ref = refs
    high = jnp.concatenate([ah_ref[to], bh_ref[to]], axis=0)
    low = jnp.concatenate([al_ref[to], bl_ref[to]], axis=0)
    return mul3((yh_ref[...], yl_ref[...]), (high, low), NN)


def trail_cost(rows, tiles):
    return pl.CostEstimate(flops=6 * rows * NB * tiles * 128, transcendentals=0, bytes_accessed=(8 * rows + 4 * NB) * tiles * 128)


def trail_first(sensitivity, own_tile, solved, halves):
    rows, tiles, width = sensitivity.shape
    group = 8

    def kernel(sens_ref, own_ref, *refs):
        refs, out_ref = refs[:-1], refs[-1]
        sens_ref = sens_ref.reshape(rows * group, width)
        first = pl.program_id(0) == 0
        for b in range(0, group, 2):
            to = (slice(None), pl.ds(b * width, 2 * width))
            parts = []
            for c in (b, b + 1):
                part = sens_ref[pl.ds(c, rows, stride=group), :]
                if c == 0:
                    part = jnp.where(first, own_ref[...], part)
                parts.append(part)
            out_ref[to] = jnp.concatenate(parts, axis=1) - trail_change(refs, to)

    wide = group * width
    return pl.pallas_call(
        kernel,
        grid=(tiles // group,),
        out_shape=pltpu.HBM((rows, tiles * width), F32),
        in_specs=[
            pl.BlockSpec((rows, group, width), lambda i: (0, i, 0)),
            pl.BlockSpec((rows, width), lambda i: (0, 0)),
            *trail_specs(rows, wide, True),
        ],
        out_specs=pl.BlockSpec((rows, wide), lambda i: (0, i)),
        compiler_params=pltpu.CompilerParams(vmem_limit_bytes=24 * MIB),
        cost_estimate=trail_cost(rows, tiles),
        name="trail_first",
    )(*in_hbm([sensitivity]), own_tile, *solved, *in_hbm(halves))


def trail_second(partial, solved, halves, tiles):
    rows = partial.shape[0]
    width = 128
    group = 8

    def kernel(in_ref, *refs):
        refs, out_ref = refs[:-1], refs[-1].reshape(rows * group, width)
        for b in range(0, group, 2):
            to = (slice(None), pl.ds(b * width, 2 * width))
            value = in_ref[to] - trail_change(refs, to)
            out_ref[pl.ds(b, rows, stride=group), :] = value[:, :width]
            out_ref[pl.ds(b + 1, rows, stride=group), :] = value[:, width:]

    wide = group * width
    return pl.pallas_call(
        kernel,
        grid=(tiles // group,),
        out_shape=jax.ShapeDtypeStruct((rows, tiles, width), F32),
        in_specs=[pl.BlockSpec((rows, wide), lambda i: (0, i)), *trail_specs(rows, wide, False)],
        out_specs=pl.BlockSpec((rows, group, width), lambda i: (0, i, 0)),
        compiler_params=pltpu.CompilerParams(vmem_limit_bytes=24 * MIB),
        cost_estimate=trail_cost(rows, tiles),
        name="trail_second",
    )(*in_hbm([partial, *solved, *halves]))


def place_unknowns(core, parts):
    rows, half = parts[0].shape
    per_step = half // 128
    cycles = 2 * per_step

    def kernel(core_ref, *refs):
        out_ref = refs[-1].reshape(rows * cycles, 128)
        own = pl.program_id(0) == core_ref[0]
        for chosen, wanted in ((refs[0:2], own), (refs[2:4], jnp.logical_not(own))):

            @pl.when(wanted)
            def _(chosen=chosen):
                for step in range(2):
                    for a in range(per_step):
                        out_ref[pl.ds(step * per_step + a, rows, stride=cycles), :] = chosen[step][:, pl.ds(a * 128, 128)]

    spec = pl.BlockSpec((rows, half), lambda i, core_ref: (0, 0))
    return pl.pallas_call(
        kernel,
        out_shape=jax.ShapeDtypeStruct((2 * rows, cycles, 128), F32),
        grid_spec=pltpu.PrefetchScalarGridSpec(
            num_scalar_prefetch=1,
            grid=(2,),
            in_specs=[spec] * 4,
            out_specs=pl.BlockSpec((rows, cycles, 128), lambda i, core_ref: (i, 0, 0)),
        ),
        compiler_params=pltpu.CompilerParams(vmem_limit_bytes=18 * MIB),
        name="place_unknowns",
    )(core, parts[0], parts[2], parts[1], parts[3])


def shards(factor_rows, sensitivity, pivots):
    count = lax.axis_size("pcol")
    sizes = grid_of(count)
    cycles, width, col_tiles = factor_rows.shape[:3]
    rows = sensitivity.shape[0]
    per_block = NB // width
    half = NB // 2
    quarter = half // 2
    index = lax.axis_index("pcol")
    core = lax.axis_index("prow")
    tiles = source_tiles(sizes, index)
    swap = lambda value: lax.ppermute(value, "prow", [(0, 1), (1, 0)])
    step_z = lambda value: shift(value, sizes, 0, 1)
    keep = jnp.stack([index >= per_block, index >= 2 * per_block]).astype(jnp.int32)
    own_columns = lax.dynamic_slice(pivots, (index * width,), (width,))

    stripe_layers = [lax.optimization_barrier(sensitivity[:, 0, :])]
    stripe_layers.append(step_z(stripe_layers[0]))
    corner = factor_rows[:, :, 0, :].reshape(cycles * width, width)
    partners = [(j, j + per_block) for j in range(per_block)] + [(j + per_block, j) for j in range(per_block)]
    shared = jnp.concatenate([corner[quarter:half], corner[half + quarter :]], axis=0)
    received = lax.ppermute(shared, "pcol", partners)
    other_rows = swap(factor_rows)
    across = gather_across(stripe_layers[:1], sizes)
    own0 = prepare(factor_rows, keep, 0, "prepare_own_first")
    first = index < per_block
    diag0 = [jnp.where(first, corner[:quarter], received[:quarter])]
    late = [
        jnp.concatenate(
            [
                jnp.where(first, received[:quarter], corner[:quarter]),
                jnp.where(first, received[quarter:], corner[half : half + quarter]),
            ],
            axis=0,
        )
    ]
    stripe_layers[1], across, keep, diag0[0], late[0] = gate((stripe_layers[1], across, keep, diag0[0], late[0]), own0)

    stripe_layers.append(step_z(stripe_layers[1]))
    arrays = [gather_along(across, sizes)]
    diag0.append(step_z(diag0[0]))
    across = gather_across(stripe_layers[1:2], sizes)
    own1 = prepare(factor_rows, keep, 1, "prepare_own_second")
    stripe_layers[2], across, keep, diag0[1], late[0] = gate((stripe_layers[2], across, keep, diag0[1], late[0]), own1)

    stripe_layers.append(step_z(stripe_layers[2]))
    arrays.append(gather_along(across, sizes))
    diag0.append(step_z(diag0[1]))
    across = gather_across(stripe_layers[2:3], sizes)
    late.append(step_z(late[0]))
    stripe_layers[3], across, keep, diag0[2], late[1] = gate(
        (stripe_layers[3], across, keep, diag0[2], late[1]), arrays[0]
    )

    arrays.append(gather_along(across, sizes))
    across = gather_across(stripe_layers[3:4], sizes)
    diag0.append(step_z(diag0[2]))
    late.append(step_z(late[1]))
    other0 = prepare(other_rows, keep, 0, "prepare_other_first")
    across, keep, diag0[3], late[2] = gate((across, keep, diag0[3], late[2]), arrays[1], other0)

    arrays.append(gather_along(across, sizes))
    late.append(step_z(late[2]))
    diag_across = gather_across(diag0, sizes)
    other1 = prepare(other_rows, keep, 1, "prepare_other_second")
    diag_across, late[3], pivots = gate((diag_across, late[3], pivots), arrays, other1)

    diag_arrays = gather_along(diag_across, sizes)
    late_across = gather_across(late, sizes)
    stripe_places = [p for d in range(sizes[0]) for p in gathered_places(d, 1, rows // 2, sizes)]
    stripe_arrays = [array for layer in arrays for array in layer]
    wanted = jnp.concatenate([pivots[: 2 * NB], own_columns])
    rhs0, rhs1, own_tile = permute_columns(stripe_arrays, stripe_places, rows // 2, sizes, tiles, wanted, rows)
    late_across, diag_arrays = gate((late_across, diag_arrays), rhs0)

    late_arrays = gather_along(late_across, sizes)
    own_diag, diag_places = end_to_end(diag_arrays, gathered_places(0, sizes[0], quarter // 2, sizes))

    def first_rows(tile, row):
        return tile < 2 * per_block, tile % per_block, row + jnp.where(tile < per_block, 0, quarter)

    def second_rows(tile, row):
        return tile < 2 * per_block, tile % per_block, row + jnp.where(tile < per_block, quarter, 0)

    own_y0, other_y0, *y0 = solve(
        tiles, rhs0, sizes, ([(own_diag, swap(own_diag))], [diag_places], quarter // 2, first_rows), "solve_first"
    )
    partial = trail_first(sensitivity, own_tile, y0, (*own0, *other0))
    swapped_y0 = swap(other_y0)

    ups = sizes[1]
    held = (0, ups)
    early = {k: swap(late_arrays[k]) for k in held}
    late_arrays, early, rhs1, swapped_y0 = gate((late_arrays, early, rhs1, swapped_y0), partial)
    pairs = [(array, early[k] if k in held else swap(array)) for k, array in enumerate(late_arrays)]
    late_places = gathered_places(0, sizes[0], quarter, sizes)
    couple_group = (pairs[:ups], late_places[:ups], quarter, second_rows)
    second_group = (
        pairs[ups:],
        [[(start, row - quarter, place) for start, row, place in inner] for inner in late_places[ups:]],
        quarter,
        second_rows,
    )
    rhs1 = couple(tiles, rhs1, sizes, y0, couple_group, None)
    own_y1, other_y1, *y1 = solve(tiles, rhs1, sizes, second_group, "solve_second", to_hbm=True)
    updated = trail_second(partial, y1, (*own1, *other1), col_tiles)

    adjoint = place_unknowns(core.reshape(1).astype(jnp.int32), [own_y0, swapped_y0, own_y1, swap(other_y1)])
    return adjoint, updated


def solution(mesh):
    return jax.shard_map(
        shards,
        mesh=mesh,
        in_specs=(P(None, "prow", None, "pcol"), P("prow", None, "pcol"), P()),
        out_specs=(P(None, None, "prow"), P("prow", None, "pcol")),
        check_vma=False,
    )
```

```python
import functools

import jax
import jax.numpy as jnp
from jax import lax
from jax.experimental import pallas as pl
from jax.experimental.pallas import tpu as pltpu
from jax.sharding import PartitionSpec as P

NB = 1024
F32 = jnp.float32
BF16 = jnp.bfloat16
MIB = 1024 * 1024


def grid_of(count):
    z_size = 4
    side = 1
    while side * side * z_size < count:
        side += 1
    return z_size, side, side


def split(value):
    high = value.astype(BF16)
    return high, (value - high.astype(F32)).astype(BF16)


NN = ((1,), (0,))
NT = ((1,), (1,))


def mul3(left, right, dims):
    left = jnp.concatenate([left[0], left[0], left[1]], axis=1)
    right = jnp.concatenate([right[0], right[1], right[0]], axis=dims[1][0])
    return lax.dot_general(left, right, (dims, ((), ())), preferred_element_type=F32)


def gate(wanted, *others):
    return lax.optimization_barrier((wanted, others))[0]


def shift(value, sizes, axis, step):
    z_size, y_size, x_size = sizes
    pairs = []
    for z in range(z_size):
        for y in range(y_size):
            for x in range(x_size):
                at = [z, y, x]
                to = list(at)
                to[axis] = (at[axis] + step) % sizes[axis]
                pairs.append(tuple((c[0] * y_size + c[1]) * x_size + c[2] for c in (at, to)))
    return lax.ppermute(value, "pcol", pairs)


def ring(value, sizes, axis):
    held = [value]
    for _ in range(sizes[axis] - 1):
        held.append(shift(held[-1], sizes, axis, 1))
    return held


def gather_across(layers, sizes):
    half = layers[0].shape[0] // 2
    upper = jnp.concatenate([held[:half] for held in layers], axis=0)
    lower = jnp.concatenate([held[half:] for held in layers], axis=0)
    return jnp.concatenate(ring(upper, sizes, 2), axis=0), jnp.concatenate(ring(lower, sizes, 1), axis=0)


def gather_along(across, sizes):
    return ring(across[0], sizes, 1) + ring(across[1], sizes, 2)


def gathered_places(first_layer, layers, half, sizes):
    places = []
    for dy in range(sizes[1]):
        inner = [((dx * layers + d) * half, 0, (first_layer + d, dy, dx)) for dx in range(sizes[2]) for d in range(layers)]
        places.append(inner)
    for dx in range(sizes[2]):
        inner = [((dy * layers + d) * half, half, (first_layer + d, dy, dx)) for dy in range(sizes[1]) for d in range(layers)]
        places.append(inner)
    return places


def end_to_end(arrays, places):
    inner, base = [], 0
    for array, own in zip(arrays, places, strict=True):
        inner += [(base + start, first, place) for start, first, place in own]
        base += array.shape[0]
    return jnp.concatenate(arrays, axis=0), inner


def source_tiles(sizes, index):
    z_size, y_size, x_size = sizes
    z, y, x = index // (y_size * x_size), index // x_size % y_size, index % x_size
    places = jnp.arange(z_size * y_size * x_size)
    dz, dy, dx = places // (y_size * x_size), places // x_size % y_size, places % x_size
    return ((z - dz) % z_size * y_size + (y - dy) % y_size) * x_size + (x - dx) % x_size


def slot_of(place, sizes):
    return (place[0] * sizes[1] + place[1]) * sizes[2] + place[2]


def permute_columns(arrays, places, half, sizes, tiles, wanted, rows):
    count = sizes[0] * sizes[1] * sizes[2]
    width = wanted.shape[0]
    step = 256
    depth = count * 128

    def kernel(tiles_ref, wanted_ref, *refs):
        parts, outs, (both_ref, hot_ref) = refs[:-5], refs[-5:-2], refs[-2:]
        for part, inner in zip(parts, places, strict=True):
            for start, first, place in inner:
                high, low = split(part[pl.ds(start, half), :])
                lanes = pl.ds(slot_of(place, sizes) * 128, 128)
                both_ref[pl.ds(first, half), lanes] = high
                both_ref[pl.ds(rows + first, half), lanes] = low
        def pick(start, size, out_ref, to):
            columns = wanted_ref[:, pl.ds(start, size)]
            lane = lax.broadcasted_iota(jnp.int32, (128, size), 0)
            for slot in range(count):
                hot = (columns - tiles_ref[slot] * 128) == lane
                hot_ref[pl.ds(slot * 128, 128), pl.ds(0, size)] = hot.astype(F32).astype(BF16)
            got = jnp.dot(both_ref[...], hot_ref[:, pl.ds(0, size)], preferred_element_type=F32)
            out_ref[:, pl.ds(to, size)] = got[:rows] + got[rows:]

        for k in range(2):

            @pl.loop(0, NB // step, unroll=NB // step if depth <= 2 * NB else 1)
            def _(i, k=k):
                to = pl.multiple_of(i * step, step)
                pick(k * NB + to, step, outs[k], to)

        pick(2 * NB, width - 2 * NB, outs[2], 0)

    vmem = pl.BlockSpec(memory_space=pltpu.VMEM)
    return pl.pallas_call(
        kernel,
        out_shape=[jax.ShapeDtypeStruct((rows, size), F32) for size in (NB, NB, width - 2 * NB)],
        in_specs=[pl.BlockSpec(memory_space=pltpu.SMEM), vmem] + [vmem] * len(arrays),
        out_specs=[vmem] * 3,
        scratch_shapes=[pltpu.VMEM((2 * rows, depth), BF16), pltpu.VMEM((depth, step), BF16)],
        compiler_params=pltpu.CompilerParams(vmem_limit_bytes=22 * MIB),
        cost_estimate=pl.CostEstimate(flops=4 * rows * depth * width, transcendentals=0, bytes_accessed=8 * rows * depth),
        name="permute_columns",
    )(tiles, wanted.reshape(1, width), *arrays)


def in_hbm(arrays):
    return [pltpu.with_memory_space_constraint(array, pltpu.HBM) for array in arrays]


def prepare(block, keep, step, name):
    cycles, depth, tiles, width = block.shape
    cycles //= 2

    def kernel(keep_ref, in_ref, high_ref, low_ref):
        own = keep_ref[step]
        for b in range(tiles):
            value = in_ref[0, pl.ds(b, depth, stride=tiles), :]
            if b == 0:
                value = jnp.where(own > 0, value, jnp.zeros_like(value))
            high, low = split(value)
            high_ref[:, pl.ds(b * width, width)] = high
            low_ref[:, pl.ds(b * width, width)] = low

    out = pltpu.HBM((cycles * depth, tiles * width), BF16)
    spec = pl.BlockSpec((depth, tiles * width), lambda a: (a, 0))
    return pl.pallas_call(
        kernel,
        grid=(cycles,),
        out_shape=(out, out),
        in_specs=[
            pl.BlockSpec(memory_space=pltpu.SMEM),
            pl.BlockSpec((1, depth * tiles, width), lambda a: (a + step * cycles, 0, 0)),
        ],
        out_specs=(spec, spec),
        compiler_params=pltpu.CompilerParams(vmem_limit_bytes=12 * MIB),
        cost_estimate=pl.CostEstimate(flops=0, transcendentals=0, bytes_accessed=12 * cycles * depth * tiles * width),
        name=name,
    )(keep, *in_hbm([block.reshape(2 * cycles, depth * tiles, width)]))


def load_blocks(group, tiles_ref, parts, sizes, high_ref, low_ref):
    arrays, places, size, where = group
    half = NB // 2
    at = 0
    for pair, inner in zip(arrays, places, strict=True):
        for side in range(len(pair)):
            part = parts[at]
            if len(part.shape) == 3:
                part = part.reshape(part.shape[0] * part.shape[1], 128)
            at += 1
            for start, first, place in inner:
                belongs, tile, row = where(tiles_ref[slot_of(place, sizes)], first)

                def put(part=part, start=start, tile=tile, row=row, side=side):
                    high, low = split(part[pl.ds(start, size), :])
                    rows_to = pl.ds(pl.multiple_of(row + side * half, 128), size)
                    high_ref[tile, rows_to, :] = high
                    low_ref[tile, rows_to, :] = low

                if sizes[0] * sizes[1] * sizes[2] * 128 <= 2 * NB:
                    put()
                else:
                    pl.when(belongs)(put)


def block_specs(operands, chosen):
    if chosen is None:
        return [pl.BlockSpec(memory_space=pltpu.VMEM)] * len(operands)
    chips, depth, width = operands[0].shape
    spec = pl.BlockSpec((chips, depth // 2, width), lambda i: (0, chosen, 0), pipeline_mode=pl.Buffered(1))
    return [spec] * len(operands)


def solve(tiles, rhs, sizes, diagonal, name, chosen=None, to_hbm=False):
    rows = rhs.shape[0]
    per_block = NB // 128
    half = NB // 2
    step = 256
    operands = [array for pair in diagonal[0] for array in pair]

    def kernel(tiles_ref, rhs_ref, *refs):
        parts = refs[: len(operands)]
        own_ref, other_ref, out_high, out_low, high_ref, low_ref = refs[len(operands) :]
        load_blocks(diagonal, tiles_ref, parts, sizes, high_ref, low_ref)
        left = split(rhs_ref[...])
        for start in range(0, NB, step):
            wanted = pl.ds(start, step)
            right = tuple(jnp.concatenate([r[t, wanted, :] for t in range(per_block)], axis=1) for r in (high_ref, low_ref))
            value = mul3(left, right, NT)
            out_high[:, wanted], out_low[:, wanted] = split(value)
            to = own_ref if start < half else other_ref
            to[:, pl.ds(start % half, step)] = value

    vmem = pl.BlockSpec(memory_space=pltpu.VMEM)
    f32 = jax.ShapeDtypeStruct((rows, half), F32)
    b16 = jax.ShapeDtypeStruct((rows, NB), BF16)
    halves_spec = vmem
    if to_hbm:
        b16 = pltpu.HBM((rows, NB), BF16)
        halves_spec = pl.BlockSpec((rows, NB), lambda i: (0, 0), pipeline_mode=pl.Buffered(1))
    return pl.pallas_call(
        kernel,
        out_shape=(f32, f32, b16, b16),
        grid=(1,),
        in_specs=[pl.BlockSpec(memory_space=pltpu.SMEM), vmem, *block_specs(operands, chosen)],
        out_specs=(vmem, vmem, halves_spec, halves_spec),
        scratch_shapes=[pltpu.VMEM((per_block, NB, 128), BF16)] * 2,
        compiler_params=pltpu.CompilerParams(vmem_limit_bytes=24 * MIB),
        cost_estimate=pl.CostEstimate(flops=6 * rows * NB * NB, transcendentals=0, bytes_accessed=8 * NB * NB),
        name=name,
    )(tiles, rhs, *operands)


def couple(tiles, rhs, sizes, solved, coupling, chosen):
    rows = rhs.shape[0]
    per_block = NB // 128
    operands = [array for pair in coupling[0] for array in pair]

    def kernel(tiles_ref, rhs_ref, yh_ref, yl_ref, *refs):
        parts, (out_ref, high_ref, low_ref) = refs[: len(operands)], refs[len(operands) :]
        load_blocks(coupling, tiles_ref, parts, sizes, high_ref, low_ref)
        left = (yh_ref[...], yl_ref[...])
        for t in range(0, per_block, 2):
            to = (slice(None), pl.ds(t * 128, 256))
            right = tuple(jnp.concatenate([r[t], r[t + 1]], axis=1) for r in (high_ref, low_ref))
            out_ref[to] = rhs_ref[to] - mul3(left, right, NN)

    vmem = pl.BlockSpec(memory_space=pltpu.VMEM)
    return pl.pallas_call(
        kernel,
        out_shape=jax.ShapeDtypeStruct((rows, NB), F32),
        grid=(1,),
        in_specs=[pl.BlockSpec(memory_space=pltpu.SMEM), vmem, vmem, vmem, *block_specs(operands, chosen)],
        out_specs=vmem,
        scratch_shapes=[pltpu.VMEM((per_block, NB, 128), BF16)] * 2,
        compiler_params=pltpu.CompilerParams(vmem_limit_bytes=22 * MIB),
        cost_estimate=pl.CostEstimate(flops=6 * rows * NB * NB, transcendentals=0, bytes_accessed=8 * NB * NB),
        name="couple",
    )(tiles, rhs, *solved, *operands)


def trail_specs(rows, wide, in_vmem):
    whole = pl.BlockSpec((rows, NB), lambda i: (0, 0), pipeline_mode=pl.Buffered(1))
    if in_vmem:
        whole = pl.BlockSpec(memory_space=pltpu.VMEM)
    part = pl.BlockSpec((NB // 2, wide), lambda i: (0, i))
    return [whole, whole, part, part, part, part]


def trail_change(refs, to):
    yh_ref, yl_ref, ah_ref, al_ref, bh_ref, bl_ref = refs
    high = jnp.concatenate([ah_ref[to], bh_ref[to]], axis=0)
    low = jnp.concatenate([al_ref[to], bl_ref[to]], axis=0)
    return mul3((yh_ref[...], yl_ref[...]), (high, low), NN)


def trail_cost(rows, tiles):
    return pl.CostEstimate(flops=6 * rows * NB * tiles * 128, transcendentals=0, bytes_accessed=(8 * rows + 4 * NB) * tiles * 128)


def trail_first(sensitivity, own_tile, solved, halves):
    rows, tiles, width = sensitivity.shape
    group = 8

    def kernel(sens_ref, own_ref, *refs):
        refs, out_ref = refs[:-1], refs[-1]
        sens_ref = sens_ref.reshape(rows * group, width)
        first = pl.program_id(0) == 0
        for b in range(0, group, 2):
            to = (slice(None), pl.ds(b * width, 2 * width))
            parts = []
            for c in (b, b + 1):
                part = sens_ref[pl.ds(c, rows, stride=group), :]
                if c == 0:
                    part = jnp.where(first, own_ref[...], part)
                parts.append(part)
            out_ref[to] = jnp.concatenate(parts, axis=1) - trail_change(refs, to)

    wide = group * width
    return pl.pallas_call(
        kernel,
        grid=(tiles // group,),
        out_shape=pltpu.HBM((rows, tiles * width), F32),
        in_specs=[
            pl.BlockSpec((rows, group, width), lambda i: (0, i, 0)),
            pl.BlockSpec((rows, width), lambda i: (0, 0)),
            *trail_specs(rows, wide, True),
        ],
        out_specs=pl.BlockSpec((rows, wide), lambda i: (0, i)),
        compiler_params=pltpu.CompilerParams(vmem_limit_bytes=24 * MIB),
        cost_estimate=trail_cost(rows, tiles),
        name="trail_first",
    )(*in_hbm([sensitivity]), own_tile, *solved, *in_hbm(halves))


def trail_second(partial, solved, halves, tiles):
    rows = partial.shape[0]
    width = 128
    group = 8

    def kernel(in_ref, *refs):
        refs, out_ref = refs[:-1], refs[-1].reshape(rows * group, width)
        for b in range(0, group, 2):
            to = (slice(None), pl.ds(b * width, 2 * width))
            value = in_ref[to] - trail_change(refs, to)
            out_ref[pl.ds(b, rows, stride=group), :] = value[:, :width]
            out_ref[pl.ds(b + 1, rows, stride=group), :] = value[:, width:]

    wide = group * width
    return pl.pallas_call(
        kernel,
        grid=(tiles // group,),
        out_shape=jax.ShapeDtypeStruct((rows, tiles, width), F32),
        in_specs=[pl.BlockSpec((rows, wide), lambda i: (0, i)), *trail_specs(rows, wide, False)],
        out_specs=pl.BlockSpec((rows, group, width), lambda i: (0, i, 0)),
        compiler_params=pltpu.CompilerParams(vmem_limit_bytes=24 * MIB),
        cost_estimate=trail_cost(rows, tiles),
        name="trail_second",
    )(*in_hbm([partial, *solved, *halves]))


def place_unknowns(core, parts):
    rows, half = parts[0].shape
    per_step = half // 128
    cycles = 2 * per_step

    def kernel(core_ref, *refs):
        out_ref = refs[-1].reshape(rows * cycles, 128)
        own = pl.program_id(0) == core_ref[0]
        for chosen, wanted in ((refs[0:2], own), (refs[2:4], jnp.logical_not(own))):

            @pl.when(wanted)
            def _(chosen=chosen):
                for step in range(2):
                    for a in range(per_step):
                        out_ref[pl.ds(step * per_step + a, rows, stride=cycles), :] = chosen[step][:, pl.ds(a * 128, 128)]

    spec = pl.BlockSpec((rows, half), lambda i, core_ref: (0, 0))
    return pl.pallas_call(
        kernel,
        out_shape=jax.ShapeDtypeStruct((2 * rows, cycles, 128), F32),
        grid_spec=pltpu.PrefetchScalarGridSpec(
            num_scalar_prefetch=1,
            grid=(2,),
            in_specs=[spec] * 4,
            out_specs=pl.BlockSpec((rows, cycles, 128), lambda i, core_ref: (i, 0, 0)),
        ),
        compiler_params=pltpu.CompilerParams(vmem_limit_bytes=18 * MIB),
        name="place_unknowns",
    )(core, parts[0], parts[2], parts[1], parts[3])


def shards(factor_rows, sensitivity, pivots):
    count = lax.axis_size("pcol")
    sizes = grid_of(count)
    cycles, width, col_tiles = factor_rows.shape[:3]
    rows = sensitivity.shape[0]
    per_block = NB // width
    half = NB // 2
    quarter = half // 2
    index = lax.axis_index("pcol")
    core = lax.axis_index("prow")
    tiles = source_tiles(sizes, index)
    swap = lambda value: lax.ppermute(value, "prow", [(0, 1), (1, 0)])
    step_z = lambda value: shift(value, sizes, 0, 1)
    keep = jnp.stack([index >= per_block, index >= 2 * per_block]).astype(jnp.int32)
    own_columns = lax.dynamic_slice(pivots, (index * width,), (width,))

    stripe_layers = [lax.optimization_barrier(sensitivity[:, 0, :])]
    stripe_layers.append(step_z(stripe_layers[0]))
    corner = factor_rows[:, :, 0, :].reshape(cycles * width, width)
    partners = [(j, j + per_block) for j in range(per_block)] + [(j + per_block, j) for j in range(per_block)]
    shared = jnp.concatenate([corner[quarter:half], corner[half + quarter :]], axis=0)
    received = lax.ppermute(shared, "pcol", partners)
    other_rows = swap(factor_rows)
    across = gather_across(stripe_layers[:1], sizes)
    own0 = prepare(factor_rows, keep, 0, "prepare_own_first")
    first = index < per_block
    diag0 = [jnp.where(first, corner[:quarter], received[:quarter])]
    late = [
        jnp.concatenate(
            [
                jnp.where(first, received[:quarter], corner[:quarter]),
                jnp.where(first, received[quarter:], corner[half : half + quarter]),
            ],
            axis=0,
        )
    ]
    stripe_layers[1], across, keep = gate((stripe_layers[1], across, keep), own0)

    stripe_layers.append(step_z(stripe_layers[1]))
    arrays = [gather_along(across, sizes)]
    diag0.append(step_z(diag0[0]))
    across = gather_across(stripe_layers[1:2], sizes)
    own1 = prepare(factor_rows, keep, 1, "prepare_own_second")
    stripe_layers[2], across, keep, diag0[1], late[0] = gate((stripe_layers[2], across, keep, diag0[1], late[0]), own1)

    stripe_layers.append(step_z(stripe_layers[2]))
    arrays.append(gather_along(across, sizes))
    diag0.append(step_z(diag0[1]))
    across = gather_across(stripe_layers[2:3], sizes)
    late.append(step_z(late[0]))
    stripe_layers[3], across, keep, diag0[2], late[1] = gate(
        (stripe_layers[3], across, keep, diag0[2], late[1]), arrays[0]
    )

    arrays.append(gather_along(across, sizes))
    across = gather_across(stripe_layers[3:4], sizes)
    diag0.append(step_z(diag0[2]))
    late.append(step_z(late[1]))
    other0 = prepare(other_rows, keep, 0, "prepare_other_first")
    across, keep, diag0[3], late[2] = gate((across, keep, diag0[3], late[2]), arrays[1], other0)

    arrays.append(gather_along(across, sizes))
    late.append(step_z(late[2]))
    diag_across = gather_across(diag0, sizes)
    other1 = prepare(other_rows, keep, 1, "prepare_other_second")
    diag_across, late[3], pivots = gate((diag_across, late[3], pivots), arrays, other1)

    diag_arrays = gather_along(diag_across, sizes)
    late_across = gather_across(late, sizes)
    stripe_places = [p for d in range(sizes[0]) for p in gathered_places(d, 1, rows // 2, sizes)]
    stripe_arrays = [array for layer in arrays for array in layer]
    wanted = jnp.concatenate([pivots[: 2 * NB], own_columns])
    rhs0, rhs1, own_tile = permute_columns(stripe_arrays, stripe_places, rows // 2, sizes, tiles, wanted, rows)
    late_across, diag_arrays = gate((late_across, diag_arrays), rhs0)

    late_arrays = gather_along(late_across, sizes)
    own_diag, diag_places = end_to_end(diag_arrays, gathered_places(0, sizes[0], quarter // 2, sizes))

    def first_rows(tile, row):
        return tile < 2 * per_block, tile % per_block, row + jnp.where(tile < per_block, 0, quarter)

    def second_rows(tile, row):
        return tile < 2 * per_block, tile % per_block, row + jnp.where(tile < per_block, quarter, 0)

    own_y0, other_y0, *y0 = solve(
        tiles, rhs0, sizes, ([(own_diag, swap(own_diag))], [diag_places], quarter // 2, first_rows), "solve_first"
    )
    partial = trail_first(sensitivity, own_tile, y0, (*own0, *other0))
    swapped_y0 = swap(other_y0)

    ups = sizes[1]
    held = (0, ups)
    early = {k: swap(late_arrays[k]) for k in held}
    late_arrays, early, rhs1, swapped_y0 = gate((late_arrays, early, rhs1, swapped_y0), partial)
    pairs = [(array, early[k] if k in held else swap(array)) for k, array in enumerate(late_arrays)]
    late_places = gathered_places(0, sizes[0], quarter, sizes)
    couple_group = (pairs[:ups], late_places[:ups], quarter, second_rows)
    second_group = (
        pairs[ups:],
        [[(start, row - quarter, place) for start, row, place in inner] for inner in late_places[ups:]],
        quarter,
        second_rows,
    )
    rhs1 = couple(tiles, rhs1, sizes, y0, couple_group, None)
    own_y1, other_y1, *y1 = solve(tiles, rhs1, sizes, second_group, "solve_second", to_hbm=True)
    updated = trail_second(partial, y1, (*own1, *other1), col_tiles)

    adjoint = place_unknowns(core.reshape(1).astype(jnp.int32), [own_y0, swapped_y0, own_y1, swap(other_y1)])
    return adjoint, updated


def solution(mesh):
    return jax.shard_map(
        shards,
        mesh=mesh,
        in_specs=(P(None, "prow", None, "pcol"), P("prow", None, "pcol"), P()),
        out_specs=(P(None, None, "prow"), P("prow", None, "pcol")),
        check_vma=False,
    )
```
